32 devices in a mesh: dp: 2 (over core), seq: 4 (over z), head: 4 (over y, x).
Axes of the slice: x: 2, y: 2, z: 4, core: 2. Of those that a mesh axis runs over, the one named last changes fastest.
Arguments:
- x_in: bfloat16 [2, 2048, 8192], P('dp', 'seq', 'head'), may hold values from -6 to 6
- b_in: bfloat16 [2, 2048, 128], P('dp', 'seq'), may hold values from -0.06591797 to 0.06591797
- c_in: bfloat16 [2, 2048, 128], P('dp', 'seq'), may hold values from -6 to 6
- rates: float32 [2, 128, 2048], P('dp', 'head', 'seq'), may hold values from 0 to 1, as said below
- skip: float32 [128], P('head'), may hold values from 0.1 to 1.9
- doc_lengths: int32 [2, 8], P('dp'), may hold values from 1 to 1536, 2048 in all within a row
- grad_y: bfloat16 [2, 2048, 8192], P('dp', ('seq', 'head')), may hold values from -6 to 6
Outputs:
- y_out: bfloat16 [2, 2048, 8192], P('dp', 'seq', 'head')
- grad_x: bfloat16 [2, 2048, 8192], P('dp', 'seq', 'head')
- grad_skip: float32 [128], P('head')
The draws below stay inside these ranges and needn't reach their ends.
Inputs may be any that keep to these rules, and one draw needn't show every extreme that they name: rates are positive. `doc_lengths`: each row sums to 2048, and its largest entry is exactly 1536.
All inputs are finite; a program needn't handle non-finite values.
Results may differ from the reference program's by a relative error of at most 0.0024.
Values may be sent and summed in bfloat16 or wider, within the bound.
A program may use at most 128 MiB of HBM per device.

```python
import math
import jax
import jax.numpy as jnp
import numpy as np
from jax import lax

HEADS = 128
HEAD_DIM = 64
STATE = 128
GROUP = 128
DOCS = 8
TOK_DEV = 512
PACKED_BATCH = 2
PACKED_LENGTH = 2048


def draw_rates(key, part):
    key_base, key_factor, random_key_location, key_amount = jax.random.split(jax.random.fold_in(key, 17), 4)
    minimum_value = 0.1 / PACKED_LENGTH
    highest = 0.03
    spread = jax.random.uniform(key_base, (PACKED_BATCH, HEADS, 1), jnp.float32)
    base = jnp.exp(jnp.log(minimum_value) + spread * (jnp.log(highest) - jnp.log(minimum_value)))
    factor = jnp.exp(jax.random.uniform(key_factor, (PACKED_BATCH, HEADS, PACKED_LENGTH), jnp.float32, jnp.log(0.5), jnp.log(2.0)))
    break_location = jax.random.randint(random_key_location, (PACKED_BATCH, 4), 0, PACKED_LENGTH)
    token_positions = jnp.arange(PACKED_LENGTH)
    document_break = jnp.any(token_positions[None, :, None] == break_location[:, None, :], axis=-1)
    amount = jax.random.uniform(key_amount, (PACKED_BATCH, 1, PACKED_LENGTH), jnp.float32, 0.22, 0.7)
    return (base * factor + jnp.where(document_break[:, None, :], amount, 0.0)).astype(jnp.float32)


def steps_of(stream_key, dims, cuts, smallest, largest):
    gain, own = 1.0, jax.random.fold_in(stream_key, 6)
    for position, parts in cuts:
        draws = jnp.exp(jax.random.uniform(jax.random.fold_in(own, position), (parts,), jnp.float32, smallest / len(cuts), largest / len(cuts)))
        gain = gain * jnp.repeat(draws, dims[position] // parts).reshape([-1 if axis == position else 1 for axis in range(len(dims))])
    return gain


def profile(count, total, reach, lean):
    loads = [(1 << 20) // math.isqrt(standing ** lean) + 1 for standing in range(2, count + 1)]
    rest, holding = total - reach - (count - 1), [1] * (count - 1)
    while rest > 0:
        movable = [i for i in range(count - 1) if holding[i] < reach]
        mass, budget = sum([loads[i] for i in movable]), rest
        for i in movable:
            addition = min(reach - holding[i], max(1, budget * loads[i] // mass), rest)
            holding[i] = holding[i] + addition
            rest = rest - addition
    return np.array([reach] + holding)


def uneven(stream_key, count, total, most, lean):
    if count == 2:
        one = jax.random.randint(stream_key, (), max(1, total - most), min(most, total - 1) + 1)
        return jnp.stack([one, total - one])
    tallies = jnp.asarray(profile(count, total, most, lean), jnp.int32)
    couples = (count - 1) // 2
    donor, taker = tallies[1:1 + 2 * couples:2], tallies[2:2 + 2 * couples:2]
    margin = jnp.minimum(donor - 1, most - taker)
    passed = jax.random.randint(jax.random.fold_in(stream_key, 1), (couples,), 0, 1 << 20) % (margin + 1)
    tallies = tallies.at[1:1 + 2 * couples:2].set(donor - passed).at[2:2 + 2 * couples:2].set(taker + passed)
    return tallies[jax.random.permutation(jax.random.fold_in(stream_key, 2), count)]


def centred(rng, dims, deviation, limit, cuts=(), kind=jnp.bfloat16):
    drawn = deviation * jax.random.normal(rng, dims, jnp.float32)
    if cuts:
        drawn = drawn * steps_of(rng, dims, cuts, -0.22, 0.18)
    return jnp.clip(drawn, -limit, limit).astype(kind)


def setup_inputs(seed: int = 0) -> dict:
    key_of = jax.random.split(jax.random.key(seed), 8)
    x_in = centred(key_of[0], (PACKED_BATCH, PACKED_LENGTH, HEADS * HEAD_DIM), 1.0, 6.0, ((0, 2), (1, 4), (2, 4)))
    b_in = centred(key_of[1], (PACKED_BATCH, PACKED_LENGTH, STATE), (0.125 / STATE ** 0.5), 0.06591797, ((0, 2), (1, 4)))
    c_in = centred(key_of[2], (PACKED_BATCH, PACKED_LENGTH, STATE), 1.0, 6.0, ((0, 2), (1, 4)))
    rates = draw_rates(jax.random.fold_in(key_of[7], 71), 0)
    skip = jnp.clip(1.0 + 0.18 * jax.random.normal(key_of[4], (HEADS,), jnp.float32), 0.1, 1.9)
    doc_lengths = jax.vmap(lambda own: uneven(own, DOCS, PACKED_LENGTH, 3 * TOK_DEV, 2))(jax.random.split(key_of[5], PACKED_BATCH)).reshape((PACKED_BATCH, DOCS)).astype(jnp.int32)
    grad_y = centred(key_of[6], (PACKED_BATCH, PACKED_LENGTH, HEADS * HEAD_DIM), 1.0, 6.0, ((0, 2), (1, 16)))
    return {"x_in": x_in, "b_in": b_in, "c_in": c_in, "rates": rates, "skip": skip, "doc_lengths": doc_lengths, "grad_y": grad_y}


def block_terms(b_rows, c_rows, rate_rows, doc_rows, prev_doc):
    running = jnp.cumsum(rate_rows, axis=1)
    inner = jnp.dot(c_rows, b_rows.T, preferred_element_type=jnp.float32)
    order = jnp.arange(doc_rows.shape[0], dtype=jnp.int32)
    same_doc = (doc_rows[:, None] == doc_rows[None, :]) & (order[:, None] >= order[None, :])
    gaps = running[:, :, None] - running[:, None, :]
    weights = jnp.exp(-jnp.where(same_doc[None], gaps, 1e+30))
    scores = (weights * inner[None]).astype(jnp.bfloat16)
    to_end = jnp.where((doc_rows == doc_rows[-1])[None], jnp.exp(-(running[:, -1:] - running)), 0.0)
    from_prev = jnp.where((doc_rows == prev_doc)[None], jnp.exp(-running), 0.0)
    return (scores, to_end, from_prev)

def forward_block(carried_state, inputs_block):
    x_rows, b_rows, c_rows, scores, to_end, from_prev, end_prev = inputs_block
    inside = jnp.einsum('hts,shp->thp', scores.astype(jnp.float32), x_rows.astype(jnp.float32))
    carried = from_prev.T[:, :, None] * jnp.einsum('tn,hnp->thp', c_rows.astype(jnp.float32), carried_state, precision=lax.Precision.HIGHEST)
    weighted = to_end[:, :, None] * b_rows.astype(jnp.float32)[None]
    updated = end_prev[:, None, None] * carried_state + jnp.einsum('hsn,shp->hnp', weighted, x_rows.astype(jnp.float32), precision=lax.Precision.HIGHEST)
    return (updated, inside + carried)

def backward_block(adjoint, inputs_block):
    g_rows, b_rows, c_rows, scores, to_end, from_prev, end_prev = inputs_block
    inside = jnp.einsum('hts,thp->shp', scores.astype(jnp.float32), g_rows.astype(jnp.float32))
    carried = to_end.T[:, :, None] * jnp.einsum('sn,hnp->shp', b_rows.astype(jnp.float32), adjoint, precision=lax.Precision.HIGHEST)
    weighted = from_prev[:, :, None] * c_rows.astype(jnp.float32)[None]
    updated = end_prev[:, None, None] * adjoint + jnp.einsum('htn,thp->hnp', weighted, g_rows.astype(jnp.float32), precision=lax.Precision.HIGHEST)
    return (updated, inside + carried)

def local_sweeps(x_heads, grad_heads, b_rows, c_rows, rate_rows, doc_rows, prev_doc):
    row_count, heads_local, head_dim = x_heads.shape
    block_count = row_count // GROUP
    state_dim = b_rows.shape[1]
    blocks_x = x_heads.reshape(block_count, GROUP, heads_local, head_dim)
    blocks_g = grad_heads.reshape(block_count, GROUP, heads_local, head_dim)
    blocks_b = b_rows.reshape(block_count, GROUP, state_dim)
    blocks_c = c_rows.reshape(block_count, GROUP, state_dim)
    blocks_rate = rate_rows.reshape(heads_local, block_count, GROUP).transpose(1, 0, 2)
    blocks_doc = doc_rows.reshape(block_count, GROUP)
    prev_docs = jnp.concatenate([prev_doc[None], blocks_doc[:-1, -1]]).astype(jnp.int32)
    scores, to_end, from_prev = jax.vmap(block_terms)(blocks_b, blocks_c, blocks_rate, blocks_doc, prev_docs)
    end_prev = from_prev[:, :, -1]
    zero_state = jnp.zeros((heads_local, state_dim, head_dim), jnp.float32)
    states_end, forward_out = lax.scan(forward_block, zero_state, (blocks_x, blocks_b, blocks_c, scores, to_end, from_prev, end_prev))
    final_adjoint, backward_out = lax.scan(backward_block, zero_state, (blocks_g, blocks_b, blocks_c, scores, to_end, from_prev, end_prev), reverse=True)
    shape_out = (row_count, heads_local, head_dim)
    return (forward_out.reshape(shape_out), states_end, backward_out.reshape(shape_out), final_adjoint)

def reference(x_in, b_in, c_in, rates, skip, doc_lengths, grad_y):

    def single_sequence(inputs_seq):
        x_rows, b_rows, c_rows, rate_rows, lengths, g_rows = inputs_seq
        seq_length = x_rows.shape[0]
        token_positions = jnp.arange(seq_length, dtype=jnp.int32)
        doc_ends = jnp.cumsum(lengths)[:-1]
        documents = lax.optimization_barrier(jnp.sum((token_positions[:, None] >= doc_ends[None, :]).astype(jnp.int32), axis=1)).astype(jnp.int32)
        x_heads = x_rows.reshape(seq_length, HEADS, HEAD_DIM)
        grad_heads = g_rows.reshape(seq_length, HEADS, HEAD_DIM)
        forward_out, states_end, backward_out, final_adjoint = local_sweeps(x_heads, grad_heads, b_rows, c_rows, rate_rows, documents, jnp.int32(-1))
        skip_gain = skip[None, :, None]
        out_values = (forward_out + skip_gain * x_heads.astype(jnp.float32)).astype(jnp.bfloat16).reshape(seq_length, -1)
        grad_values = (backward_out + skip_gain * grad_heads.astype(jnp.float32)).astype(jnp.bfloat16).reshape(seq_length, -1)
        partial_value = lax.optimization_barrier(jnp.sum(x_heads.astype(jnp.float32) * grad_heads.astype(jnp.float32), axis=(0, 2)))
        return (out_values, grad_values, partial_value)
    out_values, grad_values, per_sequence = lax.map(single_sequence, (x_in, b_in, c_in, rates, doc_lengths, grad_y))
    grad_skip = lax.optimization_barrier(jnp.sum(per_sequence, axis=0)) / jnp.sqrt(jnp.float32(PACKED_BATCH * PACKED_LENGTH * HEAD_DIM))
    return (out_values, grad_values, grad_skip)
```

```python
import functools
import math

import jax
import jax.numpy as jnp
from jax import lax
from jax.experimental import pallas as pl
from jax.experimental.pallas import tpu as pltpu
from jax.sharding import PartitionSpec as P

HEAD_DIM = 64
GROUP = 128
LANES = 128
PAIR = LANES // HEAD_DIM
HALF = GROUP // 2
EXACT = lax.Precision.HIGHEST
F32 = jnp.float32
BF16 = jnp.bfloat16
PIECES = 3
LAG_F = 2
LAG_B = 2
CHUNK = 2
OUT_COPIES = 4


def dot(a, b):
    return jnp.dot(a, b, preferred_element_type=F32)


def ndot(a, b):
    return lax.dot_general(a, b, (((1,), (1,)), ((), ())), preferred_element_type=F32)


def iota(axis, shape=(GROUP, GROUP)):
    return lax.broadcasted_iota(jnp.int32, shape, axis)


def doc_of(position, ends):
    return sum((position >= end).astype(jnp.int32) for end in ends)


def doc_ends(lengths_ref):
    ends = []
    total = jnp.int32(0)
    for k in range(lengths_ref.shape[1] - 1):
        total = total + lengths_ref[0, k]
        ends.append(total)
    return ends


def halves(value):
    high = value.astype(BF16)
    return high, (value - high.astype(F32)).astype(BF16)


def twice(value):
    return jnp.concatenate([value, value], axis=1)


def pieces(value, heads):
    copy = iota(1, value.shape) // heads
    taken = value.astype(BF16).astype(F32)
    out, rest = taken, value
    for i in range(1, PIECES):
        rest = rest - taken
        taken = rest.astype(BF16).astype(F32)
        out = jnp.where(copy == i, taken, out)
    return out.astype(BF16)


def exchange_kernel(scale, lengths_hbm, x_hbm, gy_ref, b_hbm, c_hbm, rates_hbm, skip_hbm,
                    y_ref, gx_ref, sums_ref,
                    lengths_ref, skip_ref, b_ref, c_ref, rates_ref, x_ref, g_ref, into_ref, back_ref, state_out, adjoint_out,
                    state_ref, adjoint_ref, y_part, gx_part, up_ref, down_ref, rows_ref,
                    spread_ref, rates3_ref, lf_ref, lf_low, lb_ref, lb_low, cm_ref, bm_ref,
                    lane_sums, partial_ref, gathered_ref,
                    send_f, recv_f, send_b, recv_b, send_g, recv_g, send_p, recv_p,
                    own_sem, x_sem, load_sem):
    rows, width = x_ref.shape
    blocks = rows // GROUP
    pair_count = width // LANES
    heads = rates_ref.shape[0]
    copy_heads = rates3_ref.shape[0] // PIECES
    own_rows = gy_ref.shape[0]
    count, me = lax.axis_size("seq"), lax.axis_index("seq")
    head_count, head_me = lax.axis_size("head"), lax.axis_index("head")
    later = jnp.minimum(me + 1, count - 1)
    earlier = jnp.maximum(me - 1, 0)
    first, last = me == 0, me == count - 1
    mesh_id = pl.DeviceIdType.MESH

    loads = [
        pltpu.make_async_copy(a, b, load_sem.at[i])
        for i, (a, b) in enumerate([
            (rates_hbm, rates_ref), (lengths_hbm, lengths_ref), (b_hbm, b_ref),
            (c_hbm, c_ref), (skip_hbm, skip_ref)])
    ]
    for load in loads:
        load.start()
    barrier = pltpu.get_barrier_semaphore()
    copies = lax.axis_size("dp") * count
    copy_me = lax.axis_index("dp") * count + me

    def copy_peer(i):
        other = lax.rem(copy_me + i, copies)
        return {"dp": other // count, "seq": lax.rem(other, count)}

    @pl.loop(1, head_count)
    def _(i):
        pl.semaphore_signal(
            barrier, inc=1, device_id={"head": lax.rem(head_me + i, head_count)},
            device_id_type=mesh_id)

    @pl.loop(1, copies)
    def _(i):
        pl.semaphore_signal(barrier, inc=1, device_id=copy_peer(i), device_id_type=mesh_id)

    load_x = pltpu.make_async_copy(x_hbm, x_ref, x_sem)
    load_x.start()
    own = pltpu.make_async_copy(
        gy_ref.at[:, pl.ds(pl.multiple_of(head_me * width, LANES), width)],
        g_ref.at[pl.ds(pl.multiple_of(head_me * own_rows, own_rows), own_rows)],
        own_sem,
    )
    own.start()

    pl.semaphore_wait(barrier, head_count - 1 + copies - 1)

    def part(i):
        return pltpu.make_async_remote_copy(
            src_ref=partial_ref, dst_ref=gathered_ref.at[copy_me], send_sem=send_p.at[i - 1],
            recv_sem=recv_p.at[i - 1], device_id=copy_peer(i), device_id_type=mesh_id)

    def lanes_of(q, n=1):
        return pl.ds(pl.multiple_of(q * LANES, LANES), n * LANES)

    def cotangent(i, q):
        peer = lax.rem(head_me + i, head_count)
        return pltpu.make_async_remote_copy(
            src_ref=gy_ref.at[:, pl.ds(pl.multiple_of(peer * width + q * LANES, LANES), LANES)],
            dst_ref=g_ref.at[pl.ds(pl.multiple_of(head_me * own_rows, own_rows), own_rows), lanes_of(q)],
            send_sem=send_g.at[i - 1, q], recv_sem=recv_g.at[i - 1, q],
            device_id={"head": peer}, device_id_type=mesh_id)

    def forward(q):
        return pltpu.make_async_remote_copy(
            src_ref=state_out.at[q], dst_ref=into_ref.at[q], send_sem=send_f.at[q],
            recv_sem=recv_f.at[q], device_id={"seq": later}, device_id_type=mesh_id)

    def backward(q):
        return pltpu.make_async_remote_copy(
            src_ref=adjoint_out.at[q], dst_ref=back_ref.at[q], send_sem=send_b.at[q],
            recv_sem=recv_b.at[q], device_id={"seq": earlier}, device_id_type=mesh_id)

    @pl.loop(0, pair_count)
    def _(q):
        @pl.loop(1, head_count)
        def _(i):
            cotangent(i, q).start()

    def span_of(k):
        return slice(k * GROUP, (k + 1) * GROUP)

    for load in loads:
        load.wait()
    if copy_heads > heads:
        rates3_ref[...] = jnp.zeros_like(rates3_ref)
    for i in range(PIECES):
        rates3_ref[i * copy_heads : i * copy_heads + heads] = rates_ref[...]
    lower = (iota(1) <= iota(0)).astype(F32)
    spread_shape = (PIECES * copy_heads, width)
    head_of_lane = iota(1, spread_shape) // HEAD_DIM
    row = iota(0, spread_shape)
    hit = row == head_of_lane
    for i in range(1, PIECES):
        hit = hit | (row == head_of_lane + i * copy_heads)
    spread_ref[...] = jnp.where(hit, 1.0, 0.0).astype(BF16)

    middles, totals = [], []
    for k in range(blocks):
        run = lax.dot_general(
            lower, rates3_ref[:, span_of(k)], (((1,), (1,)), ((), ())),
            precision=EXACT, preferred_element_type=F32)
        middle = run[HALF - 1 : HALF]
        middles.append(middle)
        totals.append(run[GROUP - 1 : GROUP])
        down_ref[span_of(k)] = dot(pieces(jnp.exp(middle - run), copy_heads), spread_ref[...])
        up_ref[span_of(k)] = dot(pieces(jnp.exp(run - middle), copy_heads), spread_ref[...])

    ends = doc_ends(lengths_ref)
    at = me * rows
    prev_doc = doc_of(at - 1, ends)
    last_doc = doc_of(at + rows - 1, ends)

    zero = jnp.zeros_like(totals[0])
    gaps = [middles[k] for k in range(blocks)]
    gaps += [totals[k] - middles[k] for k in range(blocks)]
    gaps += [totals[k] for k in range(blocks)]
    gaps += [sum(totals[:k], zero) for k in range(blocks)]
    gaps += [sum(totals[k + 1 :], zero) for k in range(blocks)]
    gaps += [sum(totals, zero)]
    stacked = jnp.zeros((rows_ref.shape[0], zero.shape[1]), F32)
    place = iota(0, stacked.shape)
    for i, gap in enumerate(gaps):
        stacked = jnp.where(place == i, gap, stacked)
    through = jnp.where(prev_doc == last_doc, 1.0, 0.0)
    decays = jnp.exp(-stacked)
    decays = jnp.where(place == 5 * blocks, decays * through, decays)
    rows_ref[...] = dot(pieces(decays, copy_heads), spread_ref[...])

    cols = [doc_of(at + k * GROUP + iota(0), ends) for k in range(blocks)]
    lines = [doc_of(at + k * GROUP + iota(1, (1, GROUP)), ends) for k in range(blocks)]
    for k in range(blocks):
        b, c = b_ref[span_of(k)], c_ref[span_of(k)]
        from_prev, to_last = cols[k] == prev_doc, cols[k] == last_doc
        state_dim = b.shape[1]
        cm = jnp.where(from_prev[:, :state_dim], c.astype(F32), 0.0)
        bm = jnp.where(to_last[:, :state_dim], b.astype(F32), 0.0)
        cm_ref[span_of(k)] = cm.astype(BF16)
        bm_ref[span_of(k)] = bm.astype(BF16)
        lf_ref[k, (blocks - k) * GROUP : (blocks - k + 1) * GROUP] = twice(bm.T.astype(BF16))
        lb_ref[k, (k + 1) * GROUP : (k + 2) * GROUP] = twice(cm.T.astype(BF16))
        for j in range(k + 1):
            inner = ndot(c, b_ref[span_of(j)])
            inner_t = ndot(b_ref[span_of(j)], c)
            same = cols[k] == lines[j]
            same_t = cols[j] == lines[k]
            if k == j:
                same = same & (iota(0) >= iota(1))
                same_t = same_t & (iota(0) <= iota(1))
            high, low = halves(jnp.where(same, inner, 0.0))
            lf_ref[j, span_of(k - j)] = twice(high)
            lf_low[j, span_of(k - j)] = low
            high, low = halves(jnp.where(same_t, inner_t, 0.0))
            lb_ref[k, span_of(j)] = twice(high)
            lb_low[k, span_of(j)] = low
    own.wait()
    load_x.wait()

    def gain_of(q, n):
        lane_head = iota(1, (1, n * LANES)) // HEAD_DIM
        gain = jnp.full((1, n * LANES), skip_ref[q * PAIR], F32)
        for h in range(1, n * PAIR):
            gain = jnp.where(lane_head == h, skip_ref[q * PAIR + h], gain)
        return gain

    def row_of(kind, k, lanes):
        i = kind * blocks + k
        return rows_ref[i : i + 1, lanes]

    def pairs_of(ref, q, n):
        return jnp.concatenate([ref[q + i] for i in range(n)], axis=1)

    def local_forward(q, n):
        lanes = lanes_of(q, n)
        off, diagonal, state = [None] * blocks, [None] * blocks, None
        for j in range(blocks):
            x = x_ref[span_of(j), lanes].astype(F32)
            high, low = halves(up_ref[span_of(j), lanes] * x)
            wide = dot(lf_ref[j, : (blocks - j + 1) * GROUP], jnp.concatenate([high, low], axis=0))
            fine = dot(lf_low[j, : (blocks - j) * GROUP], high)
            to_end, over = row_of(1, j, lanes), row_of(2, j, lanes)
            diagonal[j] = wide[:GROUP] + fine[:GROUP]
            for k in range(j + 1, blocks):
                tile = to_end * (wide[span_of(k - j)] + fine[span_of(k - j)])
                off[k] = tile if off[k] is None else over * off[k] + tile
            add = to_end * wide[span_of(blocks - j)]
            state = add if state is None else over * state + add
        for i in range(n):
            mine = state[:, i * LANES : (i + 1) * LANES]

            @pl.when(first)
            def _():
                into_ref[q + i] = jnp.zeros(into_ref.shape[1:], BF16)
                state_out[q + i] = mine.astype(BF16)
                forward(q + i).start()

            @pl.when(jnp.logical_not(first))
            def _():
                state_ref[q + i] = mine

        gain = gain_of(q, n)
        for k in range(blocks):
            total = diagonal[k]
            if k:
                total = total + row_of(0, k, lanes) * off[k]
            x = x_ref[span_of(k), lanes].astype(F32)
            y_part[span_of(k), lanes] = down_ref[span_of(k), lanes] * total + gain * x

    def pass_forward(q):
        @pl.when(jnp.logical_not(first))
        def _():
            forward(q).wait_recv()

            @pl.when(jnp.logical_not(last))
            def _():
                passed = row_of(5, 0, lanes_of(q)) * into_ref[q].astype(F32)
                state_out[q] = (passed + state_ref[q]).astype(BF16)
                forward(q).start()

    def finish_forward(q, n):
        lanes = lanes_of(q, n)
        carried = dot(cm_ref[...], pairs_of(into_ref, q, n))
        for k in range(blocks):
            come = down_ref[span_of(k), lanes] * row_of(0, k, lanes)
            if k:
                come = come * row_of(3, k, lanes)
            y_ref[span_of(k), lanes] = (
                y_part[span_of(k), lanes] + come * carried[span_of(k)]).astype(BF16)

    def local_backward(q, n):
        lanes = lanes_of(q, n)

        @pl.loop(1, head_count)
        def _(i):
            for more in range(n):
                cotangent(i, q + more).wait_recv()

        off, diagonal, adjoint = [None] * blocks, [None] * blocks, None
        partial = jnp.zeros((GROUP, n * LANES), F32)
        for k in reversed(range(blocks)):
            g = g_ref[span_of(k), lanes].astype(F32)
            partial = partial + x_ref[span_of(k), lanes].astype(F32) * g
            high, low = halves(down_ref[span_of(k), lanes] * g)
            wide = dot(lb_ref[k, : (k + 2) * GROUP], jnp.concatenate([high, low], axis=0))
            fine = dot(lb_low[k, : (k + 1) * GROUP], high)
            from_start, over = row_of(0, k, lanes), row_of(2, k, lanes)
            diagonal[k] = wide[span_of(k)] + fine[span_of(k)]
            for j in range(k):
                tile = from_start * (wide[span_of(j)] + fine[span_of(j)])
                off[j] = tile if off[j] is None else over * off[j] + tile
            add = from_start * wide[span_of(k + 1)]
            adjoint = add if adjoint is None else over * adjoint + add
        for i in range(n):
            mine = adjoint[:, i * LANES : (i + 1) * LANES]

            @pl.when(last)
            def _():
                back_ref[q + i] = jnp.zeros(back_ref.shape[1:], BF16)
                adjoint_out[q + i] = mine.astype(BF16)
                backward(q + i).start()

            @pl.when(jnp.logical_not(last))
            def _():
                adjoint_ref[q + i] = mine

        sums = jnp.sum(partial, axis=0, keepdims=True)
        for i in range(n):
            lane_sums[pl.ds(q + i, 1)] = sums[:, i * LANES : (i + 1) * LANES]
        gain = gain_of(q, n)
        for j in range(blocks):
            total = diagonal[j]
            if j < blocks - 1:
                total = total + row_of(1, j, lanes) * off[j]
            g = g_ref[span_of(j), lanes].astype(F32)
            gx_part[span_of(j), lanes] = up_ref[span_of(j), lanes] * total + gain * g

    def pass_backward(q):
        @pl.when(jnp.logical_not(last))
        def _():
            backward(q).wait_recv()

            @pl.when(jnp.logical_not(first))
            def _():
                passed = row_of(5, 0, lanes_of(q)) * back_ref[q].astype(F32)
                adjoint_out[q] = (passed + adjoint_ref[q]).astype(BF16)
                backward(q).start()

    def finish_backward(q, n):
        lanes = lanes_of(q, n)
        carried = dot(bm_ref[...], pairs_of(back_ref, q, n))
        for j in range(blocks):
            go = up_ref[span_of(j), lanes] * row_of(1, j, lanes)
            if j < blocks - 1:
                go = go * row_of(4, j, lanes)
            gx_ref[span_of(j), lanes] = (
                gx_part[span_of(j), lanes] + go * carried[span_of(j)]).astype(BF16)

    def send_sums():
        sums = lane_sums[...]
        lane = iota(0, (LANES, pair_count * PAIR)) // HEAD_DIM
        head = iota(1, (LANES, pair_count * PAIR))
        pick = (lane == lax.rem(head, PAIR)).astype(F32)
        by_head = lax.dot_general(sums, pick, (((1,), (0,)), ((), ())),
                                  precision=EXACT, preferred_element_type=F32)
        mine = iota(0, by_head.shape) == iota(1, by_head.shape) // PAIR
        line = jnp.sum(jnp.where(mine, by_head, 0.0), axis=0, keepdims=True)
        partial_ref[...] = jnp.broadcast_to(line, partial_ref.shape)
        gathered_ref[copy_me] = partial_ref[...]

        @pl.loop(1, copies)
        def _(i):
            part(i).start()

    n = CHUNK if pair_count % CHUNK == 0 else 1

    @pl.loop(0, pair_count // n)
    def _(i):
        local_forward(i * n, n)

    def ends_chunk(q, upto):
        return (q >= 0) & (q < upto) & (lax.rem(q, n) == n - 1)

    singles = pair_count - n

    @pl.loop(0, pair_count + max(LAG_F, LAG_B) * (count - 1))
    def _(t):
        q = t - LAG_F * me
        r = t - LAG_B * (count - 1 - me)

        @pl.when((r >= 0) & (r < pair_count))
        def _():
            pass_backward(r)

        @pl.when((q >= 0) & (q < pair_count))
        def _():
            pass_forward(q)

        @pl.when(ends_chunk(t, singles))
        def _():
            local_backward(t - (n - 1), n)

        @pl.when((t >= singles) & (t < pair_count))
        def _():
            local_backward(t, 1)

        @pl.when(t == pair_count - 1)
        def _():
            send_sums()

        @pl.when(ends_chunk(q, pair_count))
        def _():
            finish_forward(q - (n - 1), n)

        @pl.when(ends_chunk(r, singles))
        def _():
            finish_backward(r - (n - 1), n)

        @pl.when((r >= singles) & (r < pair_count))
        def _():
            finish_backward(r, 1)

    @pl.loop(0, pair_count)
    def _(q):
        @pl.loop(1, head_count)
        def _(i):
            cotangent(i, q).wait_send()

        @pl.when(jnp.logical_not(last))
        def _():
            forward(q).wait_send()

        @pl.when(jnp.logical_not(first))
        def _():
            backward(q).wait_send()

    @pl.loop(1, copies)
    def _(i):
        part(i).wait()

    total = gathered_ref[0]
    for other in range(1, copies):
        total = total + gathered_ref[other]
    sums_ref[...] = total[:1] / scale


def store_kernel(y_ref, gx_ref, sums_ref, y_out, gx_out, sums_out, sems):
    jobs = [(sums_ref, sums_out)]
    step = y_ref.shape[0] // OUT_COPIES
    for i in range(OUT_COPIES):
        span = pl.ds(i * step, step)
        jobs += [(y_ref.at[span], y_out.at[span]), (gx_ref.at[span], gx_out.at[span])]
    moves = [pltpu.make_async_copy(a, b, sems.at[i]) for i, (a, b) in enumerate(jobs)]
    for move in moves:
        move.start()
    for move in moves:
        move.wait()


def shards(x_in, b_in, c_in, rates, skip, doc_lengths, grad_y):
    _, rows, width = x_in.shape
    heads = skip.shape[0]
    state_dim = b_in.shape[2]
    pairs = width // LANES
    blocks = rows // GROUP
    peers = lax.axis_size("head") - 1
    copies = lax.axis_size("dp") * lax.axis_size("seq")
    tokens_all = copies * rows * HEAD_DIM
    copy_heads = -(-heads // 8) * 8
    vmem = pl.BlockSpec(memory_space=pltpu.VMEM)
    hbm = pl.BlockSpec(memory_space=pltpu.HBM)
    dma = pltpu.SemaphoreType.DMA
    wide = (rows, width)
    sent = pltpu.VMEM((pairs, state_dim, LANES), BF16)
    states = pltpu.VMEM((pairs, state_dim, LANES), F32)
    marks = -(-(5 * blocks + 1) // 8) * 8
    y, gx, sums = pl.pallas_call(
        functools.partial(exchange_kernel, math.sqrt(tokens_all)),
        in_specs=[hbm] * 7,
        out_specs=[vmem] * 3,
        out_shape=[pltpu.VMEM(wide, BF16), pltpu.VMEM(wide, BF16),
                   pltpu.VMEM((1, heads), F32)],
        scratch_shapes=[
            pltpu.SMEM(doc_lengths.shape, jnp.int32), pltpu.SMEM(skip.shape, F32),
            pltpu.VMEM(b_in.shape[1:], BF16), pltpu.VMEM(c_in.shape[1:], BF16),
            pltpu.VMEM(rates.shape[1:], F32),
            pltpu.VMEM(wide, BF16), pltpu.VMEM(wide, BF16), sent, sent, sent, sent,
            states, states, pltpu.VMEM(wide, F32), pltpu.VMEM(wide, F32),
            pltpu.VMEM(wide, F32), pltpu.VMEM(wide, F32), pltpu.VMEM((marks, width), F32),
            pltpu.VMEM((PIECES * copy_heads, width), BF16),
            pltpu.VMEM((PIECES * copy_heads, rows), F32),
            pltpu.VMEM((blocks, (blocks + 1) * GROUP, 2 * GROUP), BF16),
            pltpu.VMEM((blocks, blocks * GROUP, GROUP), BF16),
            pltpu.VMEM((blocks, (blocks + 1) * GROUP, 2 * GROUP), BF16),
            pltpu.VMEM((blocks, blocks * GROUP, GROUP), BF16),
            pltpu.VMEM((rows, state_dim), BF16), pltpu.VMEM((rows, state_dim), BF16),
            pltpu.VMEM((pairs, LANES), F32), pltpu.VMEM((8, heads), F32),
            pltpu.VMEM((copies, 8, heads), F32),
        ] + [dma((pairs,))] * 4 + [dma((peers, pairs))] * 2 + [dma((copies - 1,))] * 2 + [dma, dma, dma((5,))],
        compiler_params=pltpu.CompilerParams(
            collective_id=0, has_side_effects=True, vmem_limit_bytes=48 * 2**20),
        name="exchange",
    )(*[pltpu.with_memory_space_constraint(a, pltpu.HBM) for a in (
        doc_lengths, x_in[0], grad_y[0], b_in[0], c_in[0], rates[0], skip)])
    shape = jax.ShapeDtypeStruct(wide, BF16)
    y, gx, sums = pl.pallas_call(
        store_kernel,
        in_specs=[vmem] * 3,
        out_specs=[hbm] * 3,
        out_shape=[shape, shape, jax.ShapeDtypeStruct((1, heads), F32)],
        scratch_shapes=[dma((2 * OUT_COPIES + 1,))],
        compiler_params=pltpu.CompilerParams(vmem_limit_bytes=48 * 2**20),
        name="store",
    )(y, gx, sums)
    return y[None], gx[None], sums.reshape(heads)


def solution(mesh):
    placed = (
        P("dp", "seq", "head"),
        P("dp", "seq", None),
        P("dp", "seq", None),
        P("dp", "head", "seq"),
        P("head"),
        P("dp", None),
        P("dp", ("seq", "head"), None),
    )
    return jax.shard_map(
        shards,
        mesh=mesh,
        in_specs=placed,
        out_specs=(P("dp", "seq", "head"), P("dp", "seq", "head"), P("head")),
        check_vma=False,
    )
```

```python
import functools
import math

import jax
import jax.numpy as jnp
from jax import lax
from jax.experimental import pallas as pl
from jax.experimental.pallas import tpu as pltpu
from jax.sharding import PartitionSpec as P

HEAD_DIM = 64
GROUP = 128
LANES = 128
PAIR = LANES // HEAD_DIM
HALF = GROUP // 2
EXACT = lax.Precision.HIGHEST
F32 = jnp.float32
BF16 = jnp.bfloat16
PIECES = 3
LAG_F = 4
LAG_B = 3
CHUNK = 2
SINGLE = 4
LATE = 2
OUT_COPIES = 4


def dot(a, b):
    return jnp.dot(a, b, preferred_element_type=F32)


def ndot(a, b):
    return lax.dot_general(a, b, (((1,), (1,)), ((), ())), preferred_element_type=F32)


def iota(axis, shape=(GROUP, GROUP)):
    return lax.broadcasted_iota(jnp.int32, shape, axis)


def doc_of(position, ends):
    return sum((position >= end).astype(jnp.int32) for end in ends)


def doc_ends(lengths_ref):
    ends = []
    total = jnp.int32(0)
    for k in range(lengths_ref.shape[1] - 1):
        total = total + lengths_ref[0, k]
        ends.append(total)
    return ends


def halves(value):
    high = value.astype(BF16)
    return high, (value - high.astype(F32)).astype(BF16)


def twice(value):
    return jnp.concatenate([value, value], axis=1)


def pieces(value, heads):
    copy = iota(1, value.shape) // heads
    taken = value.astype(BF16).astype(F32)
    out, rest = taken, value
    for i in range(1, PIECES):
        rest = rest - taken
        taken = rest.astype(BF16).astype(F32)
        out = jnp.where(copy == i, taken, out)
    return out.astype(BF16)


def exchange_kernel(scale, lengths_hbm, x_hbm, gy_ref, b_hbm, c_hbm, rates_hbm, skip_hbm,
                    y_ref, gx_ref, sums_ref,
                    lengths_ref, skip_ref, b_ref, c_ref, rates_ref, x_ref, g_ref, into_ref, back_ref, far_ref, own_decay, their_decay, state_out, adjoint_out,
                    state_ref, adjoint_ref, y_part, gx_part, up_ref, down_ref, rows_ref,
                    spread_ref, rates3_ref, lf_ref, lf_low, lb_ref, lb_low, cm_ref, bm_ref,
                    lane_sums, partial_ref, gathered_ref,
                    send_f, recv_f, send_b, recv_b, send_g, recv_g, send_p, recv_p, send_x, recv_x, send_d, recv_d,
                    own_sem, x_sem, load_sem):
    rows, width = x_ref.shape
    blocks = rows // GROUP
    pair_count = width // LANES
    heads = rates_ref.shape[0]
    copy_heads = rates3_ref.shape[0] // PIECES
    own_rows = gy_ref.shape[0]
    count, me = lax.axis_size("seq"), lax.axis_index("seq")
    head_count, head_me = lax.axis_size("head"), lax.axis_index("head")
    later = jnp.minimum(me + 1, count - 1)
    earlier = jnp.maximum(me - 1, 0)
    first, last = me == 0, me == count - 1
    mesh_id = pl.DeviceIdType.MESH

    loads = [
        pltpu.make_async_copy(a, b, load_sem.at[i])
        for i, (a, b) in enumerate([
            (rates_hbm, rates_ref), (lengths_hbm, lengths_ref), (b_hbm, b_ref),
            (c_hbm, c_ref), (skip_hbm, skip_ref)])
    ]
    for load in loads:
        load.start()
    barrier = pltpu.get_barrier_semaphore()
    copies = lax.axis_size("dp") * count
    copy_me = lax.axis_index("dp") * count + me

    def copy_peer(i):
        other = lax.rem(copy_me + i, copies)
        return {"dp": other // count, "seq": lax.rem(other, count)}

    @pl.loop(1, head_count)
    def _(i):
        pl.semaphore_signal(
            barrier, inc=1, device_id={"head": lax.rem(head_me + i, head_count)},
            device_id_type=mesh_id)

    @pl.loop(1, copies)
    def _(i):
        pl.semaphore_signal(barrier, inc=1, device_id=copy_peer(i), device_id_type=mesh_id)

    load_x = pltpu.make_async_copy(x_hbm, x_ref, x_sem)
    load_x.start()
    own = pltpu.make_async_copy(
        gy_ref.at[:, pl.ds(pl.multiple_of(head_me * width, LANES), width)],
        g_ref.at[pl.ds(pl.multiple_of(head_me * own_rows, own_rows), own_rows)],
        own_sem,
    )
    own.start()

    pl.semaphore_wait(barrier, head_count - 1 + copies - 1)

    def part(i):
        return pltpu.make_async_remote_copy(
            src_ref=partial_ref, dst_ref=gathered_ref.at[copy_me], send_sem=send_p.at[i - 1],
            recv_sem=recv_p.at[i - 1], device_id=copy_peer(i), device_id_type=mesh_id)

    def lanes_of(q, n=1):
        return pl.ds(pl.multiple_of(q * LANES, LANES), n * LANES)

    def cotangent(i, q):
        peer = lax.rem(head_me + i, head_count)
        return pltpu.make_async_remote_copy(
            src_ref=gy_ref.at[:, pl.ds(pl.multiple_of(peer * width + q * LANES, LANES), LANES)],
            dst_ref=g_ref.at[pl.ds(pl.multiple_of(head_me * own_rows, own_rows), own_rows), lanes_of(q)],
            send_sem=send_g.at[i - 1, q], recv_sem=recv_g.at[i - 1, q],
            device_id={"head": peer}, device_id_type=mesh_id)

    def forward(q):
        return pltpu.make_async_remote_copy(
            src_ref=state_out.at[q], dst_ref=into_ref.at[q], send_sem=send_f.at[q],
            recv_sem=recv_f.at[q], device_id={"seq": later}, device_id_type=mesh_id)

    def backward(q):
        return pltpu.make_async_remote_copy(
            src_ref=adjoint_out.at[q], dst_ref=back_ref.at[q], send_sem=send_b.at[q],
            recv_sem=recv_b.at[q], device_id={"seq": earlier}, device_id_type=mesh_id)

    late = min(LATE, pair_count) if count == 4 else 0
    edge = pair_count - late

    def far(q):
        return pltpu.make_async_remote_copy(
            src_ref=adjoint_out.at[q], dst_ref=far_ref.at[q - edge],
            send_sem=send_x.at[q - edge], recv_sem=recv_x.at[q - edge],
            device_id={"seq": jnp.maximum(me - 2, 0)}, device_id_type=mesh_id)

    def decay_copy():
        return pltpu.make_async_remote_copy(
            src_ref=own_decay, dst_ref=their_decay, send_sem=send_d, recv_sem=recv_d,
            device_id={"seq": earlier}, device_id_type=mesh_id)

    @pl.loop(0, pair_count)
    def _(q):
        @pl.loop(1, head_count)
        def _(i):
            cotangent(i, q).start()

    def span_of(k):
        return slice(k * GROUP, (k + 1) * GROUP)

    for load in loads:
        load.wait()
    if copy_heads > heads:
        rates3_ref[...] = jnp.zeros_like(rates3_ref)
    for i in range(PIECES):
        rates3_ref[i * copy_heads : i * copy_heads + heads] = rates_ref[...]
    lower = (iota(1) <= iota(0)).astype(F32)
    spread_shape = (PIECES * copy_heads, width)
    head_of_lane = iota(1, spread_shape) // HEAD_DIM
    row = iota(0, spread_shape)
    hit = row == head_of_lane
    for i in range(1, PIECES):
        hit = hit | (row == head_of_lane + i * copy_heads)
    spread_ref[...] = jnp.where(hit, 1.0, 0.0).astype(BF16)

    middles, totals = [], []
    for k in range(blocks):
        run = lax.dot_general(
            lower, rates3_ref[:, span_of(k)], (((1,), (1,)), ((), ())),
            precision=EXACT, preferred_element_type=F32)
        middle = run[HALF - 1 : HALF]
        middles.append(middle)
        totals.append(run[GROUP - 1 : GROUP])
        down_ref[span_of(k)] = dot(pieces(jnp.exp(middle - run), copy_heads), spread_ref[...])
        up_ref[span_of(k)] = dot(pieces(jnp.exp(run - middle), copy_heads), spread_ref[...])

    ends = doc_ends(lengths_ref)
    at = me * rows
    prev_doc = doc_of(at - 1, ends)
    last_doc = doc_of(at + rows - 1, ends)

    zero = jnp.zeros_like(totals[0])
    gaps = [middles[k] for k in range(blocks)]
    gaps += [totals[k] - middles[k] for k in range(blocks)]
    gaps += [totals[k] for k in range(blocks)]
    gaps += [sum(totals[:k], zero) for k in range(blocks)]
    gaps += [sum(totals[k + 1 :], zero) for k in range(blocks)]
    gaps += [sum(totals, zero)]
    stacked = jnp.zeros((rows_ref.shape[0], zero.shape[1]), F32)
    place = iota(0, stacked.shape)
    for i, gap in enumerate(gaps):
        stacked = jnp.where(place == i, gap, stacked)
    through = jnp.where(prev_doc == last_doc, 1.0, 0.0)
    decays = jnp.exp(-stacked)
    decays = jnp.where(place == 5 * blocks, decays * through, decays)
    rows_ref[...] = dot(pieces(decays, copy_heads), spread_ref[...])

    if late:
        @pl.when(me == 1)
        def _():
            whole = rows_ref[5 * blocks : 5 * blocks + 1, edge * LANES :]
            own_decay[...] = jnp.broadcast_to(whole, own_decay.shape)
            decay_copy().start()

    state_dim = b_ref.shape[1]
    cols = [doc_of(at + k * GROUP + iota(0), ends) for k in range(blocks)]
    lines = [doc_of(at + k * GROUP + iota(1, (1, GROUP)), ends) for k in range(blocks)]
    for k in range(blocks):
        b, c = b_ref[span_of(k)], c_ref[span_of(k)]
        from_prev, to_last = cols[k] == prev_doc, cols[k] == last_doc
        cm = jnp.where(from_prev[:, :state_dim], c.astype(F32), 0.0)
        bm = jnp.where(to_last[:, :state_dim], b.astype(F32), 0.0)
        cm_ref[span_of(k)] = cm.astype(BF16)
        bm_ref[span_of(k)] = bm.astype(BF16)
        lf_ref[k, (blocks - k) * GROUP : (blocks - k + 1) * GROUP] = twice(bm.T.astype(BF16))
        lb_ref[k, (k + 1) * GROUP : (k + 2) * GROUP] = twice(cm.T.astype(BF16))
        for j in range(k + 1):
            inner = ndot(c, b_ref[span_of(j)])
            inner_t = ndot(b_ref[span_of(j)], c)
            same = cols[k] == lines[j]
            same_t = cols[j] == lines[k]
            if k == j:
                same = same & (iota(0) >= iota(1))
                same_t = same_t & (iota(0) <= iota(1))
            high, low = halves(jnp.where(same, inner, 0.0))
            lf_ref[j, span_of(k - j)] = twice(high)
            lf_low[j, span_of(k - j)] = low
            high, low = halves(jnp.where(same_t, inner_t, 0.0))
            lb_ref[k, span_of(j)] = twice(high)
            lb_low[k, span_of(j)] = low
    own.wait()
    load_x.wait()

    def gain_of(q, n):
        lane_head = iota(1, (1, n * LANES)) // HEAD_DIM
        gain = jnp.full((1, n * LANES), skip_ref[q * PAIR], F32)
        for h in range(1, n * PAIR):
            gain = jnp.where(lane_head == h, skip_ref[q * PAIR + h], gain)
        return gain

    def row_of(kind, k, lanes):
        i = kind * blocks + k
        return rows_ref[i : i + 1, lanes]

    def pairs_of(ref, q, n):
        return jnp.concatenate([ref[q + i] for i in range(n)], axis=1)

    def local_forward(q, n):
        lanes = lanes_of(q, n)
        off, diagonal, state = [None] * blocks, [None] * blocks, None
        for j in range(blocks):
            x = x_ref[span_of(j), lanes].astype(F32)
            high, low = halves(up_ref[span_of(j), lanes] * x)
            wide = dot(lf_ref[j, : (blocks - j + 1) * GROUP], jnp.concatenate([high, low], axis=0))
            fine = dot(lf_low[j, : (blocks - j) * GROUP], high)
            to_end, over = row_of(1, j, lanes), row_of(2, j, lanes)
            diagonal[j] = wide[:GROUP] + fine[:GROUP]
            for k in range(j + 1, blocks):
                tile = to_end * (wide[span_of(k - j)] + fine[span_of(k - j)])
                off[k] = tile if off[k] is None else over * off[k] + tile
            add = to_end * wide[span_of(blocks - j)]
            state = add if state is None else over * state + add
        for i in range(n):
            mine = state[:, i * LANES : (i + 1) * LANES]

            @pl.when(first)
            def _():
                into_ref[q + i] = jnp.zeros(into_ref.shape[1:], BF16)
                state_out[q + i] = mine.astype(BF16)
                forward(q + i).start()

            @pl.when(jnp.logical_not(first))
            def _():
                state_ref[q + i] = mine

        gain = gain_of(q, n)
        for k in range(blocks):
            total = diagonal[k]
            if k:
                total = total + row_of(0, k, lanes) * off[k]
            x = x_ref[span_of(k), lanes].astype(F32)
            y_part[span_of(k), lanes] = down_ref[span_of(k), lanes] * total + gain * x

    def pass_forward(q):
        @pl.when(jnp.logical_not(first))
        def _():
            forward(q).wait_recv()

            @pl.when(jnp.logical_not(last))
            def _():
                passed = row_of(5, 0, lanes_of(q)) * into_ref[q].astype(F32)
                state_out[q] = (passed + state_ref[q]).astype(BF16)
                forward(q).start()

    def finish_forward(q, n):
        lanes = lanes_of(q, n)
        carried = dot(cm_ref[...], pairs_of(into_ref, q, n))
        for k in range(blocks):
            come = down_ref[span_of(k), lanes] * row_of(0, k, lanes)
            if k:
                come = come * row_of(3, k, lanes)
            y_ref[span_of(k), lanes] = (
                y_part[span_of(k), lanes] + come * carried[span_of(k)]).astype(BF16)

    def local_backward(q, n):
        lanes = lanes_of(q, n)

        @pl.loop(1, head_count)
        def _(i):
            for more in range(n):
                cotangent(i, q + more).wait_recv()

        scaled, adjoint = [None] * blocks, None
        for k in reversed(range(blocks)):
            g = g_ref[span_of(k), lanes].astype(F32)
            high, low = halves(down_ref[span_of(k), lanes] * g)
            scaled[k] = jnp.concatenate([high, low], axis=0)
            add = row_of(0, k, lanes) * dot(lb_ref[k, span_of(k + 1)], scaled[k])
            adjoint = add if adjoint is None else row_of(2, k, lanes) * adjoint + add
        for i in range(n):
            mine = adjoint[:, i * LANES : (i + 1) * LANES]

            @pl.when(last)
            def _():
                back_ref[q + i] = jnp.zeros(back_ref.shape[1:], BF16)
                adjoint_out[q + i] = mine.astype(BF16)
                backward(q + i).start()

            @pl.when(jnp.logical_not(last))
            def _():
                adjoint_ref[q + i] = mine

            if late:
                @pl.when((me == 1) & (q + i >= edge))
                def _():
                    adjoint_out[q + i] = mine.astype(BF16)
                    backward(q + i).start()

        off, diagonal = [None] * blocks, [None] * blocks
        partial = jnp.zeros((GROUP, n * LANES), F32)
        for k in reversed(range(blocks)):
            g = g_ref[span_of(k), lanes].astype(F32)
            partial = partial + x_ref[span_of(k), lanes].astype(F32) * g
            wide = dot(lb_ref[k, : (k + 1) * GROUP], scaled[k])
            fine = dot(lb_low[k, : (k + 1) * GROUP], scaled[k][:GROUP])
            from_start, over = row_of(0, k, lanes), row_of(2, k, lanes)
            diagonal[k] = wide[span_of(k)] + fine[span_of(k)]
            for j in range(k):
                tile = from_start * (wide[span_of(j)] + fine[span_of(j)])
                off[j] = tile if off[j] is None else over * off[j] + tile
        sums = jnp.sum(partial, axis=0, keepdims=True)
        for i in range(n):
            lane_sums[pl.ds(q + i, 1)] = sums[:, i * LANES : (i + 1) * LANES]
        gain = gain_of(q, n)
        for j in range(blocks):
            total = diagonal[j]
            if j < blocks - 1:
                total = total + row_of(1, j, lanes) * off[j]
            g = g_ref[span_of(j), lanes].astype(F32)
            gx_part[span_of(j), lanes] = up_ref[span_of(j), lanes] * total + gain * g

    def pass_backward(q):
        @pl.when(jnp.logical_not(last))
        def _():
            backward(q).wait_recv()

            @pl.when(jnp.logical_not(first) & ((q < edge) | (me == 2)))
            def _():
                passed = row_of(5, 0, lanes_of(q)) * back_ref[q].astype(F32)
                adjoint_out[q] = (passed + adjoint_ref[q]).astype(BF16)
                backward(q).start()

            if late:
                @pl.when((me == 2) & (q >= edge))
                def _():
                    far(q).start()

                @pl.when(first & (q >= edge))
                def _():
                    @pl.when(q == edge)
                    def _():
                        decay_copy().wait_recv()

                    far(q).wait_recv()
                    passed = their_decay[:1, lanes_of(q - edge)] * far_ref[q - edge].astype(F32)
                    back_ref[q] = (back_ref[q].astype(F32) + passed).astype(BF16)

    def finish_backward(q, n):
        lanes = lanes_of(q, n)
        carried = dot(bm_ref[...], pairs_of(back_ref, q, n))
        for j in range(blocks):
            go = up_ref[span_of(j), lanes] * row_of(1, j, lanes)
            if j < blocks - 1:
                go = go * row_of(4, j, lanes)
            gx_ref[span_of(j), lanes] = (
                gx_part[span_of(j), lanes] + go * carried[span_of(j)]).astype(BF16)

    def send_sums():
        sums = lane_sums[...]
        lane = iota(0, (LANES, pair_count * PAIR)) // HEAD_DIM
        head = iota(1, (LANES, pair_count * PAIR))
        pick = (lane == lax.rem(head, PAIR)).astype(F32)
        by_head = lax.dot_general(sums, pick, (((1,), (0,)), ((), ())),
                                  precision=EXACT, preferred_element_type=F32)
        mine = iota(0, by_head.shape) == iota(1, by_head.shape) // PAIR
        line = jnp.sum(jnp.where(mine, by_head, 0.0), axis=0, keepdims=True)
        partial_ref[...] = jnp.broadcast_to(line, partial_ref.shape)
        gathered_ref[copy_me] = partial_ref[...]

        @pl.loop(1, copies)
        def _(i):
            part(i).start()

    n = CHUNK if pair_count % CHUNK == 0 else 1

    def ends_chunk(q, upto):
        return (q >= 0) & (q < upto) & (lax.rem(q, n) == n - 1)

    singles = max(pair_count - SINGLE, 0) // n * n
    final = pair_count - n

    steps = max(pair_count + LAG_B * (count - 1),
                pair_count // n + LAG_F * (count - 1))

    @pl.loop(0, steps)
    def _(t):
        q = (t - LAG_F * me) * n
        r = t - LAG_B * (count - 1 - me)

        @pl.when((r >= 0) & (r < pair_count))
        def _():
            pass_backward(r)

        @pl.when(t < pair_count // n)
        def _():
            local_forward(t * n, n)

        @pl.when(ends_chunk(t, singles))
        def _():
            local_backward(t - (n - 1), n)

        @pl.when((t >= singles) & (t < pair_count))
        def _():
            local_backward(t, 1)

        @pl.when(t == pair_count - 1)
        def _():
            send_sums()

        @pl.when((q >= 0) & (q < pair_count))
        def _():
            for i in range(n):
                pass_forward(q + i)
            finish_forward(q, n)

        @pl.when(ends_chunk(r, final))
        def _():
            finish_backward(r - (n - 1), n)

        @pl.when((r >= final) & (r < pair_count))
        def _():
            finish_backward(r, 1)

    @pl.loop(0, pair_count)
    def _(q):
        @pl.loop(1, head_count)
        def _(i):
            cotangent(i, q).wait_send()

        @pl.when(jnp.logical_not(last))
        def _():
            forward(q).wait_send()

        @pl.when(jnp.logical_not(first))
        def _():
            backward(q).wait_send()

    if late:
        @pl.when(me == 1)
        def _():
            decay_copy().wait_send()

        @pl.when(me == 2)
        def _():
            @pl.loop(edge, pair_count)
            def _(q):
                far(q).wait_send()

    @pl.loop(1, copies)
    def _(i):
        part(i).wait()

    total = gathered_ref[0]
    for other in range(1, copies):
        total = total + gathered_ref[other]
    sums_ref[...] = total[:1] / scale


def store_kernel(y_ref, gx_ref, sums_ref, y_out, gx_out, sums_out, sems):
    jobs = [(sums_ref, sums_out)]
    step = y_ref.shape[0] // OUT_COPIES
    for i in range(OUT_COPIES):
        span = pl.ds(i * step, step)
        jobs += [(y_ref.at[span], y_out.at[span]), (gx_ref.at[span], gx_out.at[span])]
    moves = [pltpu.make_async_copy(a, b, sems.at[i]) for i, (a, b) in enumerate(jobs)]
    for move in moves:
        move.start()
    for move in moves:
        move.wait()


def shards(x_in, b_in, c_in, rates, skip, doc_lengths, grad_y):
    _, rows, width = x_in.shape
    heads = skip.shape[0]
    state_dim = b_in.shape[2]
    pairs = width // LANES
    blocks = rows // GROUP
    peers = lax.axis_size("head") - 1
    copies = lax.axis_size("dp") * lax.axis_size("seq")
    tokens_all = copies * rows * HEAD_DIM
    copy_heads = -(-heads // 8) * 8
    vmem = pl.BlockSpec(memory_space=pltpu.VMEM)
    hbm = pl.BlockSpec(memory_space=pltpu.HBM)
    dma = pltpu.SemaphoreType.DMA
    wide = (rows, width)
    sent = pltpu.VMEM((pairs, state_dim, LANES), BF16)
    edges = pltpu.VMEM((8, min(LATE, pairs) * LANES), F32)
    states = pltpu.VMEM((pairs, state_dim, LANES), F32)
    marks = -(-(5 * blocks + 1) // 8) * 8
    y, gx, sums = pl.pallas_call(
        functools.partial(exchange_kernel, math.sqrt(tokens_all)),
        in_specs=[hbm] * 7,
        out_specs=[vmem] * 3,
        out_shape=[pltpu.VMEM(wide, BF16), pltpu.VMEM(wide, BF16),
                   pltpu.VMEM((1, heads), F32)],
        scratch_shapes=[
            pltpu.SMEM(doc_lengths.shape, jnp.int32), pltpu.SMEM(skip.shape, F32),
            pltpu.VMEM(b_in.shape[1:], BF16), pltpu.VMEM(c_in.shape[1:], BF16),
            pltpu.VMEM(rates.shape[1:], F32),
            pltpu.VMEM(wide, BF16), pltpu.VMEM(wide, BF16), sent, sent,
            pltpu.VMEM((LATE, state_dim, LANES), BF16), edges, edges, sent, sent,
            states, states, pltpu.VMEM(wide, F32), pltpu.VMEM(wide, F32),
            pltpu.VMEM(wide, F32), pltpu.VMEM(wide, F32), pltpu.VMEM((marks, width), F32),
            pltpu.VMEM((PIECES * copy_heads, width), BF16),
            pltpu.VMEM((PIECES * copy_heads, rows), F32),
            pltpu.VMEM((blocks, (blocks + 1) * GROUP, 2 * GROUP), BF16),
            pltpu.VMEM((blocks, blocks * GROUP, GROUP), BF16),
            pltpu.VMEM((blocks, (blocks + 1) * GROUP, 2 * GROUP), BF16),
            pltpu.VMEM((blocks, blocks * GROUP, GROUP), BF16),
            pltpu.VMEM((rows, state_dim), BF16), pltpu.VMEM((rows, state_dim), BF16),
            pltpu.VMEM((pairs, LANES), F32), pltpu.VMEM((8, heads), F32),
            pltpu.VMEM((copies, 8, heads), F32),
        ] + [dma((pairs,))] * 4 + [dma((peers, pairs))] * 2 + [dma((copies - 1,))] * 2 + [dma((LATE,))] * 2 + [dma, dma, dma, dma, dma((5,))],
        compiler_params=pltpu.CompilerParams(
            collective_id=0, has_side_effects=True, vmem_limit_bytes=48 * 2**20),
        name="exchange",
    )(*[pltpu.with_memory_space_constraint(a, pltpu.HBM) for a in (
        doc_lengths, x_in[0], grad_y[0], b_in[0], c_in[0], rates[0], skip)])
    shape = jax.ShapeDtypeStruct(wide, BF16)
    y, gx, sums = pl.pallas_call(
        store_kernel,
        in_specs=[vmem] * 3,
        out_specs=[hbm] * 3,
        out_shape=[shape, shape, jax.ShapeDtypeStruct((1, heads), F32)],
        scratch_shapes=[dma((2 * OUT_COPIES + 1,))],
        compiler_params=pltpu.CompilerParams(vmem_limit_bytes=48 * 2**20),
        name="store",
    )(y, gx, sums)
    return y[None], gx[None], sums.reshape(heads)


def solution(mesh):
    placed = (
        P("dp", "seq", "head"),
        P("dp", "seq", None),
        P("dp", "seq", None),
        P("dp", "head", "seq"),
        P("head"),
        P("dp", None),
        P("dp", ("seq", "head"), None),
    )
    return jax.shard_map(
        shards,
        mesh=mesh,
        in_specs=placed,
        out_specs=(P("dp", "seq", "head"), P("dp", "seq", "head"), P("head")),
        check_vma=False,
    )
```

```python
import functools
import math

import jax
import jax.numpy as jnp
from jax import lax
from jax.experimental import pallas as pl
from jax.experimental.pallas import tpu as pltpu
from jax.sharding import PartitionSpec as P

HEAD_DIM = 64
GROUP = 128
LANES = 128
PAIR = LANES // HEAD_DIM
HALF = GROUP // 2
EXACT = lax.Precision.HIGHEST
F32 = jnp.float32
BF16 = jnp.bfloat16
PIECES = 3
LAG_F = 4
LAG_B = 2
CHUNK = 2
SINGLE = 4
LATE = 2
AHEAD = 16
OUT_COPIES = 4


def dot(a, b):
    return jnp.dot(a, b, preferred_element_type=F32)


def ndot(a, b):
    return lax.dot_general(a, b, (((1,), (1,)), ((), ())), preferred_element_type=F32)


def iota(axis, shape=(GROUP, GROUP)):
    return lax.broadcasted_iota(jnp.int32, shape, axis)


def doc_of(position, ends):
    return sum((position >= end).astype(jnp.int32) for end in ends)


def doc_ends(lengths_ref):
    ends = []
    total = jnp.int32(0)
    for k in range(lengths_ref.shape[1] - 1):
        total = total + lengths_ref[0, k]
        ends.append(total)
    return ends


def halves(value):
    high = value.astype(BF16)
    return high, (value - high.astype(F32)).astype(BF16)


def twice(value):
    return jnp.concatenate([value, value], axis=1)


def pieces(value, heads):
    copy = iota(1, value.shape) // heads
    taken = value.astype(BF16).astype(F32)
    out, rest = taken, value
    for i in range(1, PIECES):
        rest = rest - taken
        taken = rest.astype(BF16).astype(F32)
        out = jnp.where(copy == i, taken, out)
    return out.astype(BF16)


def exchange_kernel(scale, lengths_hbm, x_hbm, gy_ref, b_hbm, c_hbm, rates_hbm, skip_hbm,
                    y_ref, gx_ref, sums_ref,
                    lengths_ref, skip_ref, b_ref, c_ref, rates_ref, x_ref, g_ref, into_ref, back_ref, far_ref, own_decay, their_decay, state_out, adjoint_out,
                    state_ref, adjoint_ref, y_part, gx_part, up_ref, down_ref, rows_ref,
                    spread_ref, rates3_ref, lf_ref, lf_low, lb_ref, lb_low, cm_ref, bm_ref,
                    lane_sums, partial_ref, gathered_ref,
                    send_f, recv_f, send_b, recv_b, send_g, recv_g, send_p, recv_p, send_x, recv_x, send_d, recv_d,
                    own_sem, x_sem, load_sem):
    rows, width = x_ref.shape
    blocks = rows // GROUP
    pair_count = width // LANES
    heads = rates_ref.shape[0]
    copy_heads = rates3_ref.shape[0] // PIECES
    own_rows = gy_ref.shape[0]
    count, me = lax.axis_size("seq"), lax.axis_index("seq")
    head_count, head_me = lax.axis_size("head"), lax.axis_index("head")
    later = jnp.minimum(me + 1, count - 1)
    earlier = jnp.maximum(me - 1, 0)
    first, last = me == 0, me == count - 1
    mesh_id = pl.DeviceIdType.MESH

    loads = [
        pltpu.make_async_copy(a, b, load_sem.at[i])
        for i, (a, b) in enumerate([
            (rates_hbm, rates_ref), (lengths_hbm, lengths_ref), (b_hbm, b_ref),
            (c_hbm, c_ref), (skip_hbm, skip_ref)])
    ]
    for load in loads:
        load.start()
    barrier = pltpu.get_barrier_semaphore()
    copies = lax.axis_size("dp") * count
    copy_me = lax.axis_index("dp") * count + me

    def copy_peer(i):
        other = lax.rem(copy_me + i, copies)
        return {"dp": other // count, "seq": lax.rem(other, count)}

    @pl.loop(1, head_count)
    def _(i):
        pl.semaphore_signal(
            barrier, inc=1, device_id={"head": lax.rem(head_me + i, head_count)},
            device_id_type=mesh_id)

    @pl.loop(1, copies)
    def _(i):
        pl.semaphore_signal(barrier, inc=1, device_id=copy_peer(i), device_id_type=mesh_id)

    load_x = pltpu.make_async_copy(x_hbm, x_ref, x_sem)
    load_x.start()
    own = pltpu.make_async_copy(
        gy_ref.at[:, pl.ds(pl.multiple_of(head_me * width, LANES), width)],
        g_ref.at[pl.ds(pl.multiple_of(head_me * own_rows, own_rows), own_rows)],
        own_sem,
    )
    own.start()

    pl.semaphore_wait(barrier, head_count - 1 + copies - 1)

    def part(i):
        return pltpu.make_async_remote_copy(
            src_ref=partial_ref, dst_ref=gathered_ref.at[copy_me], send_sem=send_p.at[i - 1],
            recv_sem=recv_p.at[i - 1], device_id=copy_peer(i), device_id_type=mesh_id)

    def lanes_of(q, n=1):
        return pl.ds(pl.multiple_of(q * LANES, LANES), n * LANES)

    def cotangent(i, q):
        peer = lax.rem(head_me + i, head_count)
        return pltpu.make_async_remote_copy(
            src_ref=gy_ref.at[:, pl.ds(pl.multiple_of(peer * width + q * LANES, LANES), LANES)],
            dst_ref=g_ref.at[pl.ds(pl.multiple_of(head_me * own_rows, own_rows), own_rows), lanes_of(q)],
            send_sem=send_g.at[i - 1, q], recv_sem=recv_g.at[i - 1, q],
            device_id={"head": peer}, device_id_type=mesh_id)

    def forward(q):
        return pltpu.make_async_remote_copy(
            src_ref=state_out.at[q], dst_ref=into_ref.at[q], send_sem=send_f.at[q],
            recv_sem=recv_f.at[q], device_id={"seq": later}, device_id_type=mesh_id)

    def backward(q):
        return pltpu.make_async_remote_copy(
            src_ref=adjoint_out.at[q], dst_ref=back_ref.at[q], send_sem=send_b.at[q],
            recv_sem=recv_b.at[q], device_id={"seq": earlier}, device_id_type=mesh_id)

    late = min(LATE, pair_count) if count == 4 else 0
    edge = pair_count - late

    def far(q):
        return pltpu.make_async_remote_copy(
            src_ref=adjoint_out.at[q], dst_ref=far_ref.at[q - edge],
            send_sem=send_x.at[q - edge], recv_sem=recv_x.at[q - edge],
            device_id={"seq": jnp.maximum(me - 2, 0)}, device_id_type=mesh_id)

    def decay_copy():
        return pltpu.make_async_remote_copy(
            src_ref=own_decay, dst_ref=their_decay, send_sem=send_d, recv_sem=recv_d,
            device_id={"seq": earlier}, device_id_type=mesh_id)

    def send_cotangent(q):
        @pl.loop(1, head_count)
        def _(i):
            cotangent(i, q).start()

    ahead = min(AHEAD, pair_count)

    @pl.loop(0, ahead)
    def _(q):
        send_cotangent(q)

    def span_of(k):
        return slice(k * GROUP, (k + 1) * GROUP)

    for load in loads:
        load.wait()
    if copy_heads > heads:
        rates3_ref[...] = jnp.zeros_like(rates3_ref)
    for i in range(PIECES):
        rates3_ref[i * copy_heads : i * copy_heads + heads] = rates_ref[...]
    lower = (iota(1) <= iota(0)).astype(F32)
    spread_shape = (PIECES * copy_heads, width)
    head_of_lane = iota(1, spread_shape) // HEAD_DIM
    row = iota(0, spread_shape)
    hit = row == head_of_lane
    for i in range(1, PIECES):
        hit = hit | (row == head_of_lane + i * copy_heads)
    spread_ref[...] = jnp.where(hit, 1.0, 0.0).astype(BF16)

    middles, totals = [], []
    for k in range(blocks):
        run = lax.dot_general(
            lower, rates3_ref[:, span_of(k)], (((1,), (1,)), ((), ())),
            precision=EXACT, preferred_element_type=F32)
        middle = run[HALF - 1 : HALF]
        middles.append(middle)
        totals.append(run[GROUP - 1 : GROUP])
        down_ref[span_of(k)] = dot(pieces(jnp.exp(middle - run), copy_heads), spread_ref[...])
        up_ref[span_of(k)] = dot(pieces(jnp.exp(run - middle), copy_heads), spread_ref[...])

    ends = doc_ends(lengths_ref)
    at = me * rows
    prev_doc = doc_of(at - 1, ends)
    last_doc = doc_of(at + rows - 1, ends)

    zero = jnp.zeros_like(totals[0])
    gaps = [middles[k] for k in range(blocks)]
    gaps += [totals[k] - middles[k] for k in range(blocks)]
    gaps += [totals[k] for k in range(blocks)]
    gaps += [sum(totals[:k], zero) for k in range(blocks)]
    gaps += [sum(totals[k + 1 :], zero) for k in range(blocks)]
    gaps += [sum(totals, zero)]
    stacked = jnp.zeros((rows_ref.shape[0], zero.shape[1]), F32)
    place = iota(0, stacked.shape)
    for i, gap in enumerate(gaps):
        stacked = jnp.where(place == i, gap, stacked)
    through = jnp.where(prev_doc == last_doc, 1.0, 0.0)
    decays = jnp.exp(-stacked)
    decays = jnp.where(place == 5 * blocks, decays * through, decays)
    rows_ref[...] = dot(pieces(decays, copy_heads), spread_ref[...])

    if late:
        @pl.when(me == 1)
        def _():
            whole = rows_ref[5 * blocks : 5 * blocks + 1, edge * LANES :]
            own_decay[...] = jnp.broadcast_to(whole, own_decay.shape)
            decay_copy().start()

    state_dim = b_ref.shape[1]
    cols = [doc_of(at + k * GROUP + iota(0), ends) for k in range(blocks)]
    lines = [doc_of(at + k * GROUP + iota(1, (1, GROUP)), ends) for k in range(blocks)]
    for k in range(blocks):
        b, c = b_ref[span_of(k)], c_ref[span_of(k)]
        from_prev, to_last = cols[k] == prev_doc, cols[k] == last_doc
        cm = jnp.where(from_prev[:, :state_dim], c.astype(F32), 0.0)
        bm = jnp.where(to_last[:, :state_dim], b.astype(F32), 0.0)
        cm_ref[span_of(k)] = cm.astype(BF16)
        bm_ref[span_of(k)] = bm.astype(BF16)
        lf_ref[k, (blocks - k) * GROUP : (blocks - k + 1) * GROUP] = twice(bm.T.astype(BF16))
        lb_ref[k, (k + 1) * GROUP : (k + 2) * GROUP] = twice(cm.T.astype(BF16))
        for j in range(k + 1):
            inner = ndot(c, b_ref[span_of(j)])
            inner_t = ndot(b_ref[span_of(j)], c)
            same = cols[k] == lines[j]
            same_t = cols[j] == lines[k]
            if k == j:
                same = same & (iota(0) >= iota(1))
                same_t = same_t & (iota(0) <= iota(1))
            high, low = halves(jnp.where(same, inner, 0.0))
            lf_ref[j, span_of(k - j)] = twice(high)
            lf_low[j, span_of(k - j)] = low
            high, low = halves(jnp.where(same_t, inner_t, 0.0))
            lb_ref[k, span_of(j)] = twice(high)
            lb_low[k, span_of(j)] = low
    own.wait()
    load_x.wait()

    def gain_of(q, n):
        lane_head = iota(1, (1, n * LANES)) // HEAD_DIM
        gain = jnp.full((1, n * LANES), skip_ref[q * PAIR], F32)
        for h in range(1, n * PAIR):
            gain = jnp.where(lane_head == h, skip_ref[q * PAIR + h], gain)
        return gain

    def row_of(kind, k, lanes):
        i = kind * blocks + k
        return rows_ref[i : i + 1, lanes]

    def pairs_of(ref, q, n):
        return jnp.concatenate([ref[q + i] for i in range(n)], axis=1)

    def local_forward(q, n):
        lanes = lanes_of(q, n)
        off, diagonal, state = [None] * blocks, [None] * blocks, None
        for j in range(blocks):
            x = x_ref[span_of(j), lanes].astype(F32)
            high, low = halves(up_ref[span_of(j), lanes] * x)
            wide = dot(lf_ref[j, : (blocks - j + 1) * GROUP], jnp.concatenate([high, low], axis=0))
            fine = dot(lf_low[j, : (blocks - j) * GROUP], high)
            to_end, over = row_of(1, j, lanes), row_of(2, j, lanes)
            diagonal[j] = wide[:GROUP] + fine[:GROUP]
            for k in range(j + 1, blocks):
                tile = to_end * (wide[span_of(k - j)] + fine[span_of(k - j)])
                off[k] = tile if off[k] is None else over * off[k] + tile
            add = to_end * wide[span_of(blocks - j)]
            state = add if state is None else over * state + add
        for i in range(n):
            mine = state[:, i * LANES : (i + 1) * LANES]

            @pl.when(first)
            def _():
                state_out[q + i] = mine.astype(BF16)
                forward(q + i).start()

            @pl.when(jnp.logical_not(first))
            def _():
                state_ref[q + i] = mine

        gain = gain_of(q, n)
        for k in range(blocks):
            total = diagonal[k]
            if k:
                total = total + row_of(0, k, lanes) * off[k]
            x = x_ref[span_of(k), lanes].astype(F32)
            y_part[span_of(k), lanes] = down_ref[span_of(k), lanes] * total + gain * x

    def pass_forward(q):
        @pl.when(jnp.logical_not(first))
        def _():
            forward(q).wait_recv()

            @pl.when(jnp.logical_not(last))
            def _():
                passed = row_of(5, 0, lanes_of(q)) * into_ref[q].astype(F32)
                state_out[q] = (passed + state_ref[q]).astype(BF16)
                forward(q).start()

    def finish_forward(q, n):
        lanes = lanes_of(q, n)

        @pl.when(first)
        def _():
            y_ref[:, lanes] = y_part[:, lanes].astype(BF16)

        @pl.when(jnp.logical_not(first))
        def _():
            carried = dot(cm_ref[...], pairs_of(into_ref, q, n))
            for k in range(blocks):
                come = down_ref[span_of(k), lanes] * row_of(0, k, lanes)
                if k:
                    come = come * row_of(3, k, lanes)
                y_ref[span_of(k), lanes] = (
                    y_part[span_of(k), lanes] + come * carried[span_of(k)]).astype(BF16)

    def local_backward(q, n):
        lanes = lanes_of(q, n)

        @pl.loop(1, head_count)
        def _(i):
            for more in range(n):
                cotangent(i, q + more).wait_recv()

        scaled, adjoint = [None] * blocks, None
        for k in reversed(range(blocks)):
            g = g_ref[span_of(k), lanes].astype(F32)
            high, low = halves(down_ref[span_of(k), lanes] * g)
            scaled[k] = jnp.concatenate([high, low], axis=0)
            add = row_of(0, k, lanes) * dot(lb_ref[k, span_of(k + 1)], scaled[k])
            adjoint = add if adjoint is None else row_of(2, k, lanes) * adjoint + add
        for i in range(n):
            mine = adjoint[:, i * LANES : (i + 1) * LANES]

            @pl.when(last)
            def _():
                adjoint_out[q + i] = mine.astype(BF16)
                backward(q + i).start()

            @pl.when(jnp.logical_not(last))
            def _():
                adjoint_ref[q + i] = mine

            if late:
                @pl.when((me == 1) & (q + i >= edge))
                def _():
                    adjoint_out[q + i] = mine.astype(BF16)
                    backward(q + i).start()

        off, diagonal = [None] * blocks, [None] * blocks
        partial = jnp.zeros((GROUP, n * LANES), F32)
        for k in reversed(range(blocks)):
            g = g_ref[span_of(k), lanes].astype(F32)
            partial = partial + x_ref[span_of(k), lanes].astype(F32) * g
            wide = dot(lb_ref[k, : (k + 1) * GROUP], scaled[k])
            fine = dot(lb_low[k, : (k + 1) * GROUP], scaled[k][:GROUP])
            from_start, over = row_of(0, k, lanes), row_of(2, k, lanes)
            diagonal[k] = wide[span_of(k)] + fine[span_of(k)]
            for j in range(k):
                tile = from_start * (wide[span_of(j)] + fine[span_of(j)])
                off[j] = tile if off[j] is None else over * off[j] + tile
        sums = jnp.sum(partial, axis=0, keepdims=True)
        for i in range(n):
            lane_sums[pl.ds(q + i, 1)] = sums[:, i * LANES : (i + 1) * LANES]
        gain = gain_of(q, n)
        for j in range(blocks):
            total = diagonal[j]
            if j < blocks - 1:
                total = total + row_of(1, j, lanes) * off[j]
            g = g_ref[span_of(j), lanes].astype(F32)
            gx_part[span_of(j), lanes] = up_ref[span_of(j), lanes] * total + gain * g

    def pass_backward(q):
        @pl.when(jnp.logical_not(last))
        def _():
            backward(q).wait_recv()

            @pl.when(jnp.logical_not(first) & ((q < edge) | (me == 2)))
            def _():
                passed = row_of(5, 0, lanes_of(q)) * back_ref[q].astype(F32)
                adjoint_out[q] = (passed + adjoint_ref[q]).astype(BF16)
                backward(q).start()

            if late:
                @pl.when((me == 2) & (q >= edge))
                def _():
                    far(q).start()

                @pl.when(first & (q >= edge))
                def _():
                    @pl.when(q == edge)
                    def _():
                        decay_copy().wait_recv()

                    far(q).wait_recv()
                    passed = their_decay[:1, lanes_of(q - edge)] * far_ref[q - edge].astype(F32)
                    back_ref[q] = (back_ref[q].astype(F32) + passed).astype(BF16)

    def finish_backward(q, n):
        lanes = lanes_of(q, n)

        @pl.when(last)
        def _():
            gx_ref[:, lanes] = gx_part[:, lanes].astype(BF16)

        @pl.when(jnp.logical_not(last))
        def _():
            carried = dot(bm_ref[...], pairs_of(back_ref, q, n))
            for j in range(blocks):
                go = up_ref[span_of(j), lanes] * row_of(1, j, lanes)
                if j < blocks - 1:
                    go = go * row_of(4, j, lanes)
                gx_ref[span_of(j), lanes] = (
                    gx_part[span_of(j), lanes] + go * carried[span_of(j)]).astype(BF16)

    def send_sums():
        sums = lane_sums[...]
        lane = iota(0, (LANES, pair_count * PAIR)) // HEAD_DIM
        head = iota(1, (LANES, pair_count * PAIR))
        pick = (lane == lax.rem(head, PAIR)).astype(F32)
        by_head = lax.dot_general(sums, pick, (((1,), (0,)), ((), ())),
                                  precision=EXACT, preferred_element_type=F32)
        mine = iota(0, by_head.shape) == iota(1, by_head.shape) // PAIR
        line = jnp.sum(jnp.where(mine, by_head, 0.0), axis=0, keepdims=True)
        partial_ref[...] = jnp.broadcast_to(line, partial_ref.shape)
        gathered_ref[copy_me] = partial_ref[...]

        @pl.loop(1, copies)
        def _(i):
            part(i).start()

    n = CHUNK if pair_count % CHUNK == 0 else 1

    def ends_chunk(q, upto):
        return (q >= 0) & (q < upto) & (lax.rem(q, n) == n - 1)

    singles = max(pair_count - SINGLE, 0) // n * n
    final = pair_count - n

    steps = max(pair_count + LAG_B * (count - 1),
                pair_count // n + LAG_F * (count - 1))

    @pl.loop(0, steps)
    def _(t):
        q = (t - LAG_F * me) * n
        r = t - LAG_B * (count - 1 - me)

        @pl.when(t + ahead < pair_count)
        def _():
            send_cotangent(t + ahead)

        @pl.when(t < pair_count // n)
        def _():
            local_forward(t * n, n)

        @pl.when(ends_chunk(t, singles))
        def _():
            local_backward(t - (n - 1), n)

        @pl.when((t >= singles) & (t < pair_count))
        def _():
            local_backward(t, 1)

        @pl.when(t == pair_count - 1)
        def _():
            send_sums()

        @pl.when(ends_chunk(r, singles))
        def _():
            for i in reversed(range(n)):
                pass_backward(r - i)
            finish_backward(r - (n - 1), n)

        @pl.when((r >= singles) & (r < pair_count))
        def _():
            pass_backward(r)

        @pl.when(ends_chunk(r, final) & (r >= singles))
        def _():
            finish_backward(r - (n - 1), n)

        @pl.when((r >= final) & (r < pair_count))
        def _():
            finish_backward(r, 1)

        @pl.when((q >= 0) & (q < pair_count))
        def _():
            for i in range(n):
                pass_forward(q + i)
            finish_forward(q, n)

    @pl.loop(0, pair_count)
    def _(q):
        @pl.loop(1, head_count)
        def _(i):
            cotangent(i, q).wait_send()

        @pl.when(jnp.logical_not(last))
        def _():
            forward(q).wait_send()

        @pl.when(jnp.logical_not(first))
        def _():
            backward(q).wait_send()

    if late:
        @pl.when(me == 1)
        def _():
            decay_copy().wait_send()

        @pl.when(me == 2)
        def _():
            @pl.loop(edge, pair_count)
            def _(q):
                far(q).wait_send()

    @pl.loop(1, copies)
    def _(i):
        part(i).wait()

    total = gathered_ref[0]
    for other in range(1, copies):
        total = total + gathered_ref[other]
    sums_ref[...] = total[:1] / scale


def store_kernel(y_ref, gx_ref, sums_ref, y_out, gx_out, sums_out, sems):
    jobs = [(sums_ref, sums_out)]
    step = y_ref.shape[0] // OUT_COPIES
    for i in range(OUT_COPIES):
        span = pl.ds(i * step, step)
        jobs += [(y_ref.at[span], y_out.at[span]), (gx_ref.at[span], gx_out.at[span])]
    moves = [pltpu.make_async_copy(a, b, sems.at[i]) for i, (a, b) in enumerate(jobs)]
    for move in moves:
        move.start()
    for move in moves:
        move.wait()


def shards(x_in, b_in, c_in, rates, skip, doc_lengths, grad_y):
    _, rows, width = x_in.shape
    heads = skip.shape[0]
    state_dim = b_in.shape[2]
    pairs = width // LANES
    blocks = rows // GROUP
    peers = lax.axis_size("head") - 1
    copies = lax.axis_size("dp") * lax.axis_size("seq")
    tokens_all = copies * rows * HEAD_DIM
    copy_heads = -(-heads // 8) * 8
    vmem = pl.BlockSpec(memory_space=pltpu.VMEM)
    hbm = pl.BlockSpec(memory_space=pltpu.HBM)
    dma = pltpu.SemaphoreType.DMA
    wide = (rows, width)
    sent = pltpu.VMEM((pairs, state_dim, LANES), BF16)
    edges = pltpu.VMEM((8, min(LATE, pairs) * LANES), F32)
    states = pltpu.VMEM((pairs, state_dim, LANES), F32)
    marks = -(-(5 * blocks + 1) // 8) * 8
    y, gx, sums = pl.pallas_call(
        functools.partial(exchange_kernel, math.sqrt(tokens_all)),
        in_specs=[hbm] * 7,
        out_specs=[vmem] * 3,
        out_shape=[pltpu.VMEM(wide, BF16), pltpu.VMEM(wide, BF16),
                   pltpu.VMEM((1, heads), F32)],
        scratch_shapes=[
            pltpu.SMEM(doc_lengths.shape, jnp.int32), pltpu.SMEM(skip.shape, F32),
            pltpu.VMEM(b_in.shape[1:], BF16), pltpu.VMEM(c_in.shape[1:], BF16),
            pltpu.VMEM(rates.shape[1:], F32),
            pltpu.VMEM(wide, BF16), pltpu.VMEM(wide, BF16), sent, sent,
            pltpu.VMEM((LATE, state_dim, LANES), BF16), edges, edges, sent, sent,
            states, states, pltpu.VMEM(wide, F32), pltpu.VMEM(wide, F32),
            pltpu.VMEM(wide, F32), pltpu.VMEM(wide, F32), pltpu.VMEM((marks, width), F32),
            pltpu.VMEM((PIECES * copy_heads, width), BF16),
            pltpu.VMEM((PIECES * copy_heads, rows), F32),
            pltpu.VMEM((blocks, (blocks + 1) * GROUP, 2 * GROUP), BF16),
            pltpu.VMEM((blocks, blocks * GROUP, GROUP), BF16),
            pltpu.VMEM((blocks, (blocks + 1) * GROUP, 2 * GROUP), BF16),
            pltpu.VMEM((blocks, blocks * GROUP, GROUP), BF16),
            pltpu.VMEM((rows, state_dim), BF16), pltpu.VMEM((rows, state_dim), BF16),
            pltpu.VMEM((pairs, LANES), F32), pltpu.VMEM((8, heads), F32),
            pltpu.VMEM((copies, 8, heads), F32),
        ] + [dma((pairs,))] * 4 + [dma((peers, pairs))] * 2 + [dma((copies - 1,))] * 2 + [dma((LATE,))] * 2 + [dma, dma, dma, dma, dma((5,))],
        compiler_params=pltpu.CompilerParams(
            collective_id=0, has_side_effects=True, vmem_limit_bytes=48 * 2**20),
        name="exchange",
    )(*[pltpu.with_memory_space_constraint(a, pltpu.HBM) for a in (
        doc_lengths, x_in[0], grad_y[0], b_in[0], c_in[0], rates[0], skip)])
    shape = jax.ShapeDtypeStruct(wide, BF16)
    y, gx, sums = pl.pallas_call(
        store_kernel,
        in_specs=[vmem] * 3,
        out_specs=[hbm] * 3,
        out_shape=[shape, shape, jax.ShapeDtypeStruct((1, heads), F32)],
        scratch_shapes=[dma((2 * OUT_COPIES + 1,))],
        compiler_params=pltpu.CompilerParams(vmem_limit_bytes=48 * 2**20),
        name="store",
    )(y, gx, sums)
    return y[None], gx[None], sums.reshape(heads)


def solution(mesh):
    placed = (
        P("dp", "seq", "head"),
        P("dp", "seq", None),
        P("dp", "seq", None),
        P("dp", "head", "seq"),
        P("head"),
        P("dp", None),
        P("dp", ("seq", "head"), None),
    )
    return jax.shard_map(
        shards,
        mesh=mesh,
        in_specs=placed,
        out_specs=(P("dp", "seq", "head"), P("dp", "seq", "head"), P("head")),
        check_vma=False,
    )
```

```python
import functools
import math

import jax
import jax.numpy as jnp
from jax import lax
from jax.experimental import pallas as pl
from jax.experimental.pallas import tpu as pltpu
from jax.sharding import PartitionSpec as P

HEAD_DIM = 64
GROUP = 128
LANES = 128
PAIR = LANES // HEAD_DIM
HALF = GROUP // 2
EXACT = lax.Precision.HIGHEST
F32 = jnp.float32
BF16 = jnp.bfloat16
PIECES = 3
LAG_F = 4
LAG_B = 2
CHUNK = 2
SINGLE = 6
LATE = 6
AHEAD = 16
OUT_COPIES = 4


def dot(a, b):
    return jnp.dot(a, b, preferred_element_type=F32)


def ndot(a, b):
    return lax.dot_general(a, b, (((1,), (1,)), ((), ())), preferred_element_type=F32)


def iota(axis, shape=(GROUP, GROUP)):
    return lax.broadcasted_iota(jnp.int32, shape, axis)


def doc_of(position, ends):
    return sum((position >= end).astype(jnp.int32) for end in ends)


def doc_ends(lengths_ref):
    ends = []
    total = jnp.int32(0)
    for k in range(lengths_ref.shape[1] - 1):
        total = total + lengths_ref[0, k]
        ends.append(total)
    return ends


def halves(value):
    high = value.astype(BF16)
    return high, (value - high.astype(F32)).astype(BF16)


def twice(value):
    return jnp.concatenate([value, value], axis=1)


def pieces(value, heads):
    copy = iota(1, value.shape) // heads
    taken = value.astype(BF16).astype(F32)
    out, rest = taken, value
    for i in range(1, PIECES):
        rest = rest - taken
        taken = rest.astype(BF16).astype(F32)
        out = jnp.where(copy == i, taken, out)
    return out.astype(BF16)


def exchange_kernel(scale, lengths_hbm, x_hbm, gy_ref, b_hbm, c_hbm, rates_hbm, skip_hbm,
                    y_ref, gx_ref, sums_ref,
                    lengths_ref, skip_ref, b_ref, c_ref, rates_ref, x_ref, g_ref, into_ref, back_ref, far_ref, own_decay, their_decay, state_out, adjoint_out,
                    state_ref, adjoint_ref, y_part, gx_part, up_ref, down_ref, rows_ref,
                    spread_ref, rates3_ref, lf_ref, lf_low, lb_ref, lb_low, cm_ref, bm_ref,
                    lane_sums, partial_ref, gathered_ref,
                    send_f, recv_f, send_b, recv_b, send_g, recv_g, send_p, recv_p, send_x, recv_x, send_d, recv_d,
                    own_sem, x_sem, load_sem):
    rows, width = x_ref.shape
    blocks = rows // GROUP
    pair_count = width // LANES
    heads = rates_ref.shape[0]
    copy_heads = rates3_ref.shape[0] // PIECES
    own_rows = gy_ref.shape[0]
    count, me = lax.axis_size("seq"), lax.axis_index("seq")
    head_count, head_me = lax.axis_size("head"), lax.axis_index("head")
    later = jnp.minimum(me + 1, count - 1)
    earlier = jnp.maximum(me - 1, 0)
    first, last = me == 0, me == count - 1
    mesh_id = pl.DeviceIdType.MESH

    loads = [
        pltpu.make_async_copy(a, b, load_sem.at[i])
        for i, (a, b) in enumerate([
            (rates_hbm, rates_ref), (lengths_hbm, lengths_ref), (b_hbm, b_ref),
            (c_hbm, c_ref), (skip_hbm, skip_ref)])
    ]
    for load in loads:
        load.start()
    barrier = pltpu.get_barrier_semaphore()
    copies = lax.axis_size("dp") * count
    copy_me = lax.axis_index("dp") * count + me

    def copy_peer(i):
        other = lax.rem(copy_me + i, copies)
        return {"dp": other // count, "seq": lax.rem(other, count)}

    @pl.loop(1, head_count)
    def _(i):
        pl.semaphore_signal(
            barrier, inc=1, device_id={"head": lax.rem(head_me + i, head_count)},
            device_id_type=mesh_id)

    @pl.loop(1, copies)
    def _(i):
        pl.semaphore_signal(barrier, inc=1, device_id=copy_peer(i), device_id_type=mesh_id)

    load_x = pltpu.make_async_copy(x_hbm, x_ref, x_sem)
    load_x.start()
    own = pltpu.make_async_copy(
        gy_ref.at[:, pl.ds(pl.multiple_of(head_me * width, LANES), width)],
        g_ref.at[pl.ds(pl.multiple_of(head_me * own_rows, own_rows), own_rows)],
        own_sem,
    )
    own.start()

    pl.semaphore_wait(barrier, head_count - 1 + copies - 1)

    def part(i):
        return pltpu.make_async_remote_copy(
            src_ref=partial_ref, dst_ref=gathered_ref.at[copy_me], send_sem=send_p.at[i - 1],
            recv_sem=recv_p.at[i - 1], device_id=copy_peer(i), device_id_type=mesh_id)

    def lanes_of(q, n=1):
        return pl.ds(pl.multiple_of(q * LANES, LANES), n * LANES)

    def cotangent(i, q):
        peer = lax.rem(head_me + i, head_count)
        return pltpu.make_async_remote_copy(
            src_ref=gy_ref.at[:, pl.ds(pl.multiple_of(peer * width + q * LANES, LANES), LANES)],
            dst_ref=g_ref.at[pl.ds(pl.multiple_of(head_me * own_rows, own_rows), own_rows), lanes_of(q)],
            send_sem=send_g.at[i - 1, q], recv_sem=recv_g.at[i - 1, q],
            device_id={"head": peer}, device_id_type=mesh_id)

    def forward(q):
        return pltpu.make_async_remote_copy(
            src_ref=state_out.at[q], dst_ref=into_ref.at[q], send_sem=send_f.at[q],
            recv_sem=recv_f.at[q], device_id={"seq": later}, device_id_type=mesh_id)

    def backward(q):
        return pltpu.make_async_remote_copy(
            src_ref=adjoint_out.at[q], dst_ref=back_ref.at[q], send_sem=send_b.at[q],
            recv_sem=recv_b.at[q], device_id={"seq": earlier}, device_id_type=mesh_id)

    late = min(LATE, pair_count) if count == 4 else 0
    edge = pair_count - late

    def far(q):
        return pltpu.make_async_remote_copy(
            src_ref=adjoint_out.at[q], dst_ref=far_ref.at[q - edge],
            send_sem=send_x.at[q - edge], recv_sem=recv_x.at[q - edge],
            device_id={"seq": jnp.maximum(me - 2, 0)}, device_id_type=mesh_id)

    def decay_copy():
        return pltpu.make_async_remote_copy(
            src_ref=own_decay, dst_ref=their_decay, send_sem=send_d, recv_sem=recv_d,
            device_id={"seq": earlier}, device_id_type=mesh_id)

    def send_cotangent(q):
        @pl.loop(1, head_count)
        def _(i):
            cotangent(i, q).start()

    ahead = min(AHEAD, pair_count)

    @pl.loop(0, ahead)
    def _(q):
        send_cotangent(q)

    def span_of(k):
        return slice(k * GROUP, (k + 1) * GROUP)

    for load in loads:
        load.wait()
    if copy_heads > heads:
        rates3_ref[...] = jnp.zeros_like(rates3_ref)
    for i in range(PIECES):
        rates3_ref[i * copy_heads : i * copy_heads + heads] = rates_ref[...]
    lower = (iota(1) <= iota(0)).astype(F32)
    spread_shape = (PIECES * copy_heads, width)
    head_of_lane = iota(1, spread_shape) // HEAD_DIM
    row = iota(0, spread_shape)
    hit = row == head_of_lane
    for i in range(1, PIECES):
        hit = hit | (row == head_of_lane + i * copy_heads)
    spread_ref[...] = jnp.where(hit, 1.0, 0.0).astype(BF16)

    middles, totals = [], []
    for k in range(blocks):
        run = lax.dot_general(
            lower, rates3_ref[:, span_of(k)], (((1,), (1,)), ((), ())),
            precision=EXACT, preferred_element_type=F32)
        middle = run[HALF - 1 : HALF]
        middles.append(middle)
        totals.append(run[GROUP - 1 : GROUP])
        down_ref[span_of(k)] = dot(pieces(jnp.exp(middle - run), copy_heads), spread_ref[...])
        up_ref[span_of(k)] = dot(pieces(jnp.exp(run - middle), copy_heads), spread_ref[...])

    ends = doc_ends(lengths_ref)
    at = me * rows
    prev_doc = doc_of(at - 1, ends)
    last_doc = doc_of(at + rows - 1, ends)

    zero = jnp.zeros_like(totals[0])
    gaps = [middles[k] for k in range(blocks)]
    gaps += [totals[k] - middles[k] for k in range(blocks)]
    gaps += [totals[k] for k in range(blocks)]
    gaps += [sum(totals[:k], zero) for k in range(blocks)]
    gaps += [sum(totals[k + 1 :], zero) for k in range(blocks)]
    gaps += [sum(totals, zero)]
    stacked = jnp.zeros((rows_ref.shape[0], zero.shape[1]), F32)
    place = iota(0, stacked.shape)
    for i, gap in enumerate(gaps):
        stacked = jnp.where(place == i, gap, stacked)
    through = jnp.where(prev_doc == last_doc, 1.0, 0.0)
    decays = jnp.exp(-stacked)
    decays = jnp.where(place == 5 * blocks, decays * through, decays)
    rows_ref[...] = dot(pieces(decays, copy_heads), spread_ref[...])

    if late:
        @pl.when(me == 1)
        def _():
            whole = rows_ref[5 * blocks : 5 * blocks + 1, edge * LANES :]
            own_decay[...] = jnp.broadcast_to(whole, own_decay.shape)
            decay_copy().start()

    state_dim = b_ref.shape[1]
    cols = [doc_of(at + k * GROUP + iota(0), ends) for k in range(blocks)]
    lines = [doc_of(at + k * GROUP + iota(1, (1, GROUP)), ends) for k in range(blocks)]
    for k in range(blocks):
        b, c = b_ref[span_of(k)], c_ref[span_of(k)]
        from_prev, to_last = cols[k] == prev_doc, cols[k] == last_doc
        cm = jnp.where(from_prev[:, :state_dim], c.astype(F32), 0.0)
        bm = jnp.where(to_last[:, :state_dim], b.astype(F32), 0.0)
        cm_ref[span_of(k)] = cm.astype(BF16)
        bm_ref[span_of(k)] = bm.astype(BF16)
        lf_ref[k, (blocks - k) * GROUP : (blocks - k + 1) * GROUP] = twice(bm.T.astype(BF16))
        lb_ref[k, (k + 1) * GROUP : (k + 2) * GROUP] = twice(cm.T.astype(BF16))
        for j in range(k + 1):
            inner = ndot(c, b_ref[span_of(j)])
            inner_t = ndot(b_ref[span_of(j)], c)
            same = cols[k] == lines[j]
            same_t = cols[j] == lines[k]
            if k == j:
                same = same & (iota(0) >= iota(1))
                same_t = same_t & (iota(0) <= iota(1))
            high, low = halves(jnp.where(same, inner, 0.0))
            lf_ref[j, span_of(k - j)] = twice(high)
            lf_low[j, span_of(k - j)] = low
            high, low = halves(jnp.where(same_t, inner_t, 0.0))
            lb_ref[k, span_of(j)] = twice(high)
            lb_low[k, span_of(j)] = low
    own.wait()
    load_x.wait()

    def gain_of(q, n):
        lane_head = iota(1, (1, n * LANES)) // HEAD_DIM
        gain = jnp.full((1, n * LANES), skip_ref[q * PAIR], F32)
        for h in range(1, n * PAIR):
            gain = jnp.where(lane_head == h, skip_ref[q * PAIR + h], gain)
        return gain

    def row_of(kind, k, lanes):
        i = kind * blocks + k
        return rows_ref[i : i + 1, lanes]

    def pairs_of(ref, q, n):
        return jnp.concatenate([ref[q + i] for i in range(n)], axis=1)

    def local_forward(q, n):
        lanes = lanes_of(q, n)
        off, diagonal, state = [None] * blocks, [None] * blocks, None
        for j in range(blocks):
            x = x_ref[span_of(j), lanes].astype(F32)
            high, low = halves(up_ref[span_of(j), lanes] * x)
            wide = dot(lf_ref[j, : (blocks - j + 1) * GROUP], jnp.concatenate([high, low], axis=0))
            fine = dot(lf_low[j, : (blocks - j) * GROUP], high)
            to_end, over = row_of(1, j, lanes), row_of(2, j, lanes)
            diagonal[j] = wide[:GROUP] + fine[:GROUP]
            for k in range(j + 1, blocks):
                tile = to_end * (wide[span_of(k - j)] + fine[span_of(k - j)])
                off[k] = tile if off[k] is None else over * off[k] + tile
            add = to_end * wide[span_of(blocks - j)]
            state = add if state is None else over * state + add
        for i in range(n):
            mine = state[:, i * LANES : (i + 1) * LANES]

            @pl.when(first)
            def _():
                state_out[q + i] = mine.astype(BF16)
                forward(q + i).start()

            @pl.when(jnp.logical_not(first))
            def _():
                state_ref[q + i] = mine

        gain = gain_of(q, n)
        for k in range(blocks):
            total = diagonal[k]
            if k:
                total = total + row_of(0, k, lanes) * off[k]
            x = x_ref[span_of(k), lanes].astype(F32)
            y_part[span_of(k), lanes] = down_ref[span_of(k), lanes] * total + gain * x

    def pass_forward(q):
        @pl.when(jnp.logical_not(first))
        def _():
            forward(q).wait_recv()

            @pl.when(jnp.logical_not(last))
            def _():
                passed = row_of(5, 0, lanes_of(q)) * into_ref[q].astype(F32)
                state_out[q] = (passed + state_ref[q]).astype(BF16)
                forward(q).start()

    def finish_forward(q, n):
        lanes = lanes_of(q, n)

        @pl.when(first)
        def _():
            y_ref[:, lanes] = y_part[:, lanes].astype(BF16)

        @pl.when(jnp.logical_not(first))
        def _():
            carried = dot(cm_ref[...], pairs_of(into_ref, q, n))
            for k in range(blocks):
                come = down_ref[span_of(k), lanes] * row_of(0, k, lanes)
                if k:
                    come = come * row_of(3, k, lanes)
                y_ref[span_of(k), lanes] = (
                    y_part[span_of(k), lanes] + come * carried[span_of(k)]).astype(BF16)

    def local_backward(q, n):
        lanes = lanes_of(q, n)

        @pl.loop(1, head_count)
        def _(i):
            for more in range(n):
                cotangent(i, q + more).wait_recv()

        scaled, adjoint = [None] * blocks, None
        for k in reversed(range(blocks)):
            g = g_ref[span_of(k), lanes].astype(F32)
            high, low = halves(down_ref[span_of(k), lanes] * g)
            scaled[k] = jnp.concatenate([high, low], axis=0)
            add = row_of(0, k, lanes) * dot(lb_ref[k, span_of(k + 1)], scaled[k])
            adjoint = add if adjoint is None else row_of(2, k, lanes) * adjoint + add
        for i in range(n):
            mine = adjoint[:, i * LANES : (i + 1) * LANES]

            @pl.when(last)
            def _():
                adjoint_out[q + i] = mine.astype(BF16)
                backward(q + i).start()

            @pl.when(jnp.logical_not(last))
            def _():
                adjoint_ref[q + i] = mine

            if late:
                @pl.when((me == 1) & (q + i >= edge))
                def _():
                    adjoint_out[q + i] = mine.astype(BF16)
                    backward(q + i).start()

        off, diagonal = [None] * blocks, [None] * blocks
        partial = jnp.zeros((GROUP, n * LANES), F32)
        for k in reversed(range(blocks)):
            g = g_ref[span_of(k), lanes].astype(F32)
            partial = partial + x_ref[span_of(k), lanes].astype(F32) * g
            wide = dot(lb_ref[k, : (k + 1) * GROUP], scaled[k])
            fine = dot(lb_low[k, : (k + 1) * GROUP], scaled[k][:GROUP])
            from_start, over = row_of(0, k, lanes), row_of(2, k, lanes)
            diagonal[k] = wide[span_of(k)] + fine[span_of(k)]
            for j in range(k):
                tile = from_start * (wide[span_of(j)] + fine[span_of(j)])
                off[j] = tile if off[j] is None else over * off[j] + tile
        sums = jnp.sum(partial, axis=0, keepdims=True)
        for i in range(n):
            lane_sums[pl.ds(q + i, 1)] = sums[:, i * LANES : (i + 1) * LANES]
        gain = gain_of(q, n)
        for j in range(blocks):
            total = diagonal[j]
            if j < blocks - 1:
                total = total + row_of(1, j, lanes) * off[j]
            g = g_ref[span_of(j), lanes].astype(F32)
            gx_part[span_of(j), lanes] = up_ref[span_of(j), lanes] * total + gain * g

    def pass_backward(q):
        @pl.when(jnp.logical_not(last))
        def _():
            backward(q).wait_recv()

            @pl.when(jnp.logical_not(first) & ((q < edge) | (me == 2)))
            def _():
                passed = row_of(5, 0, lanes_of(q)) * back_ref[q].astype(F32)
                adjoint_out[q] = (passed + adjoint_ref[q]).astype(BF16)
                backward(q).start()

            if late:
                @pl.when((me == 2) & (q >= edge))
                def _():
                    far(q).start()

                @pl.when(first & (q >= edge))
                def _():
                    @pl.when(q == edge)
                    def _():
                        decay_copy().wait_recv()

                    far(q).wait_recv()
                    passed = their_decay[:1, lanes_of(q - edge)] * far_ref[q - edge].astype(F32)
                    back_ref[q] = (back_ref[q].astype(F32) + passed).astype(BF16)

    def finish_backward(q, n):
        lanes = lanes_of(q, n)

        @pl.when(last)
        def _():
            gx_ref[:, lanes] = gx_part[:, lanes].astype(BF16)

        @pl.when(jnp.logical_not(last))
        def _():
            carried = dot(bm_ref[...], pairs_of(back_ref, q, n))
            for j in range(blocks):
                go = up_ref[span_of(j), lanes] * row_of(1, j, lanes)
                if j < blocks - 1:
                    go = go * row_of(4, j, lanes)
                gx_ref[span_of(j), lanes] = (
                    gx_part[span_of(j), lanes] + go * carried[span_of(j)]).astype(BF16)

    def send_sums():
        sums = lane_sums[...]
        lane = iota(0, (LANES, pair_count * PAIR)) // HEAD_DIM
        head = iota(1, (LANES, pair_count * PAIR))
        pick = (lane == lax.rem(head, PAIR)).astype(F32)
        by_head = lax.dot_general(sums, pick, (((1,), (0,)), ((), ())),
                                  precision=EXACT, preferred_element_type=F32)
        mine = iota(0, by_head.shape) == iota(1, by_head.shape) // PAIR
        line = jnp.sum(jnp.where(mine, by_head, 0.0), axis=0, keepdims=True)
        partial_ref[...] = jnp.broadcast_to(line, partial_ref.shape)
        gathered_ref[copy_me] = partial_ref[...]

        @pl.loop(1, copies)
        def _(i):
            part(i).start()

    n = CHUNK if pair_count % CHUNK == 0 else 1

    def ends_chunk(q, upto):
        return (q >= 0) & (q < upto) & (lax.rem(q, n) == n - 1)

    singles = max(pair_count - SINGLE, 0) // n * n
    final = pair_count - n

    steps = max(pair_count + LAG_B * (count - 1),
                pair_count // n + LAG_F * (count - 1))

    @pl.loop(0, steps)
    def _(t):
        q = (t - LAG_F * me) * n
        r = t - LAG_B * (count - 1 - me)

        @pl.when(t + ahead < pair_count)
        def _():
            send_cotangent(t + ahead)

        @pl.when(t < pair_count // n)
        def _():
            local_forward(t * n, n)

        @pl.when(ends_chunk(t, singles))
        def _():
            local_backward(t - (n - 1), n)

        @pl.when((t >= singles) & (t < pair_count))
        def _():
            local_backward(t, 1)

        @pl.when(t == pair_count - 1)
        def _():
            send_sums()

        @pl.when(ends_chunk(r, singles))
        def _():
            for i in reversed(range(n)):
                pass_backward(r - i)
            finish_backward(r - (n - 1), n)

        @pl.when((r >= singles) & (r < pair_count))
        def _():
            pass_backward(r)

        @pl.when(ends_chunk(r, final) & (r >= singles))
        def _():
            finish_backward(r - (n - 1), n)

        @pl.when((r >= final) & (r < pair_count))
        def _():
            finish_backward(r, 1)

        @pl.when((q >= 0) & (q < pair_count))
        def _():
            for i in range(n):
                pass_forward(q + i)
            finish_forward(q, n)

    @pl.loop(0, pair_count)
    def _(q):
        @pl.loop(1, head_count)
        def _(i):
            cotangent(i, q).wait_send()

        @pl.when(jnp.logical_not(last))
        def _():
            forward(q).wait_send()

        @pl.when(jnp.logical_not(first))
        def _():
            backward(q).wait_send()

    if late:
        @pl.when(me == 1)
        def _():
            decay_copy().wait_send()

        @pl.when(me == 2)
        def _():
            @pl.loop(edge, pair_count)
            def _(q):
                far(q).wait_send()

    @pl.loop(1, copies)
    def _(i):
        part(i).wait()

    total = gathered_ref[0]
    for other in range(1, copies):
        total = total + gathered_ref[other]
    sums_ref[...] = total[:1] / scale


def store_kernel(y_ref, gx_ref, sums_ref, y_out, gx_out, sums_out, sems):
    jobs = [(sums_ref, sums_out)]
    step = y_ref.shape[0] // OUT_COPIES
    for i in range(OUT_COPIES):
        span = pl.ds(i * step, step)
        jobs += [(y_ref.at[span], y_out.at[span]), (gx_ref.at[span], gx_out.at[span])]
    moves = [pltpu.make_async_copy(a, b, sems.at[i]) for i, (a, b) in enumerate(jobs)]
    for move in moves:
        move.start()
    for move in moves:
        move.wait()


def shards(x_in, b_in, c_in, rates, skip, doc_lengths, grad_y):
    _, rows, width = x_in.shape
    heads = skip.shape[0]
    state_dim = b_in.shape[2]
    pairs = width // LANES
    blocks = rows // GROUP
    peers = lax.axis_size("head") - 1
    copies = lax.axis_size("dp") * lax.axis_size("seq")
    tokens_all = copies * rows * HEAD_DIM
    copy_heads = -(-heads // 8) * 8
    vmem = pl.BlockSpec(memory_space=pltpu.VMEM)
    hbm = pl.BlockSpec(memory_space=pltpu.HBM)
    dma = pltpu.SemaphoreType.DMA
    wide = (rows, width)
    sent = pltpu.VMEM((pairs, state_dim, LANES), BF16)
    edges = pltpu.VMEM((8, min(LATE, pairs) * LANES), F32)
    states = pltpu.VMEM((pairs, state_dim, LANES), F32)
    marks = -(-(5 * blocks + 1) // 8) * 8
    y, gx, sums = pl.pallas_call(
        functools.partial(exchange_kernel, math.sqrt(tokens_all)),
        in_specs=[hbm] * 7,
        out_specs=[vmem] * 3,
        out_shape=[pltpu.VMEM(wide, BF16), pltpu.VMEM(wide, BF16),
                   pltpu.VMEM((1, heads), F32)],
        scratch_shapes=[
            pltpu.SMEM(doc_lengths.shape, jnp.int32), pltpu.SMEM(skip.shape, F32),
            pltpu.VMEM(b_in.shape[1:], BF16), pltpu.VMEM(c_in.shape[1:], BF16),
            pltpu.VMEM(rates.shape[1:], F32),
            pltpu.VMEM(wide, BF16), pltpu.VMEM(wide, BF16), sent, sent,
            pltpu.VMEM((LATE, state_dim, LANES), BF16), edges, edges, sent, sent,
            states, states, pltpu.VMEM(wide, F32), pltpu.VMEM(wide, F32),
            pltpu.VMEM(wide, F32), pltpu.VMEM(wide, F32), pltpu.VMEM((marks, width), F32),
            pltpu.VMEM((PIECES * copy_heads, width), BF16),
            pltpu.VMEM((PIECES * copy_heads, rows), F32),
            pltpu.VMEM((blocks, (blocks + 1) * GROUP, 2 * GROUP), BF16),
            pltpu.VMEM((blocks, blocks * GROUP, GROUP), BF16),
            pltpu.VMEM((blocks, (blocks + 1) * GROUP, 2 * GROUP), BF16),
            pltpu.VMEM((blocks, blocks * GROUP, GROUP), BF16),
            pltpu.VMEM((rows, state_dim), BF16), pltpu.VMEM((rows, state_dim), BF16),
            pltpu.VMEM((pairs, LANES), F32), pltpu.VMEM((8, heads), F32),
            pltpu.VMEM((copies, 8, heads), F32),
        ] + [dma((pairs,))] * 4 + [dma((peers, pairs))] * 2 + [dma((copies - 1,))] * 2 + [dma((LATE,))] * 2 + [dma, dma, dma, dma, dma((5,))],
        compiler_params=pltpu.CompilerParams(
            collective_id=0, has_side_effects=True, vmem_limit_bytes=48 * 2**20),
        name="exchange",
    )(*[pltpu.with_memory_space_constraint(a, pltpu.HBM) for a in (
        doc_lengths, x_in[0], grad_y[0], b_in[0], c_in[0], rates[0], skip)])
    shape = jax.ShapeDtypeStruct(wide, BF16)
    y, gx, sums = pl.pallas_call(
        store_kernel,
        in_specs=[vmem] * 3,
        out_specs=[hbm] * 3,
        out_shape=[shape, shape, jax.ShapeDtypeStruct((1, heads), F32)],
        scratch_shapes=[dma((2 * OUT_COPIES + 1,))],
        compiler_params=pltpu.CompilerParams(vmem_limit_bytes=48 * 2**20),
        name="store",
    )(y, gx, sums)
    return y[None], gx[None], sums.reshape(heads)


def solution(mesh):
    placed = (
        P("dp", "seq", "head"),
        P("dp", "seq", None),
        P("dp", "seq", None),
        P("dp", "head", "seq"),
        P("head"),
        P("dp", None),
        P("dp", ("seq", "head"), None),
    )
    return jax.shard_map(
        shards,
        mesh=mesh,
        in_specs=placed,
        out_specs=(P("dp", "seq", "head"), P("dp", "seq", "head"), P("head")),
        check_vma=False,
    )
```
